128 devices in a mesh: seq: 8 (over z, core), exp: 16 (over y, x).
Axes of the slice: x: 4, y: 4, z: 4, core: 2. Of those that a mesh axis runs over, the one named last changes fastest.
Arguments:
- attn_query: bfloat16 [2048, 6144], P('seq', 'exp'), may hold values from -6 to 6
- attn_key: bfloat16 [2048, 6144], P('seq', 'exp'), may hold values from -6 to 6
- attn_value: bfloat16 [2048, 6144], P('seq', 'exp'), may hold values from -40 to 40
- log_decay: float32 [48, 2048], P('exp', 'seq'), may hold values from -1.5 to 0
- residual: bfloat16 [2048, 6144], P('seq', 'exp'), may hold values from -6 to 6
- norm_gain: bfloat16 [6144], P('exp'), may hold values from 0.099609375 to 1.8984375
- expert_ids: int32 [2048, 2], P('seq'), may hold values from 0 to 15, as said below
- router_weight: bfloat16 [6144, 16], P(None, 'seq'), may hold values from -0.078125 to 0.078125
- gate_weight: bfloat16 [16, 6144, 4608], P('seq', None, 'exp'), may hold values from -0.078125 to 0.078125
- up_weight: bfloat16 [16, 6144, 4608], P('seq', None, 'exp'), may hold values from -0.078125 to 0.078125
- down_weight: bfloat16 [16, 4608, 6144], P('seq', 'exp'), may hold values from -0.125 to 0.125
Outputs:
- layer_out: bfloat16 [2048, 6144], P('seq', 'exp')
The draws below stay inside these ranges and needn't reach their ends.
Inputs may be any that keep to these rules, and one draw needn't show every extreme that they name: `expert_ids`: each row names two different experts. In every section of 256 consecutive rows no expert is named more than 64 times, and in every section some experts are named exactly 64 times.
All inputs are finite; a program needn't handle non-finite values.
Results may differ from the reference program's by a relative error of at most 0.017.
Values may be sent and summed in bfloat16 or wider, within the bound.
A program may use at most 192 MiB of HBM per device.

```python
import jax
import jax.numpy as jnp
from jax import lax

H = 48
DH = 128
D = 6144
FF = 4608
EXP_DEV = 2
EXPERTS = 16
TOPK = 2
SEC_TOK = 256
TOKEN_TOTAL = 2048
CAP = 64


def draw_attn_value(key, part):
    split_random_keys = jax.random.split(key, 3)
    column_scale = jnp.exp(jax.random.uniform(split_random_keys[1], (1, D), minval=0.0, maxval=jnp.log(10.0)))
    row_scale = jnp.exp(jax.random.uniform(split_random_keys[2], (TOKEN_TOTAL, 1), minval=0.0, maxval=jnp.log(10.0)))
    base_draw = jnp.clip(jax.random.normal(split_random_keys[0], (TOKEN_TOTAL, D)), -4.0, 4.0)
    return (0.1 * base_draw * column_scale * row_scale).astype(jnp.bfloat16)


def draw_log_decay(key, part):
    split_random_keys = jax.random.split(key, 6)
    fast_share = 0.5
    fast_head = jax.random.uniform(split_random_keys[0], (H, 1)) < fast_share
    fast_rate = jnp.exp(jax.random.uniform(split_random_keys[1], (H, 1), minval=jnp.log(1.0 / 50.0), maxval=jnp.log(1.0 / 30.0)))
    slow_rate = jnp.exp(jax.random.uniform(split_random_keys[2], (H, 1), minval=jnp.log(0.02 / TOKEN_TOTAL), maxval=jnp.log(0.3 / TOKEN_TOTAL)))
    baseline_rate = jnp.where(fast_head, fast_rate, slow_rate)
    jitter_level = jax.random.uniform(split_random_keys[3], (H, TOKEN_TOTAL), minval=0.5, maxval=1.5)
    spike_position = jax.random.randint(split_random_keys[4], (2, 1), 0, TOKEN_TOTAL)
    retained_fraction = jax.random.uniform(split_random_keys[5], (2, H, 1), minval=0.5, maxval=0.8)
    spike_location_mask = jnp.arange(TOKEN_TOTAL)[None, None, :] == spike_position[:, :, None]
    spike_amount = jnp.sum(jnp.where(spike_location_mask, jnp.log(retained_fraction), 0.0), axis=0)
    return (-baseline_rate * jitter_level + spike_amount).astype(jnp.float32)


def draw_expert_ids(key, part):
    sections = TOKEN_TOTAL // SEC_TOK
    entries = SEC_TOK * TOPK
    group_count = EXPERTS // EXP_DEV
    full_groups = max(1, 3 * group_count // 8)
    full_count = full_groups * EXP_DEV
    remaining = entries - full_count * CAP

    def one_section(section_key):
        first_key, second_key, third_key = jax.random.split(section_key, 3)
        group_order = jax.random.permutation(first_key, group_count).astype(jnp.int32)
        expert_order = (group_order[:, None] * EXP_DEV + jnp.arange(EXP_DEV, dtype=jnp.int32)[None, :]).reshape(-1)
        full_labels = jnp.repeat(expert_order[:full_count], CAP)
        slots = jax.random.permutation(second_key, (EXPERTS - full_count) * CAP)[:remaining]
        others = expert_order[full_count + (slots // CAP).astype(jnp.int32)]
        labels = jnp.sort(jnp.concatenate([full_labels, others]).astype(jnp.int32))
        table = labels.reshape(TOPK, SEC_TOK).T
        row_order = jax.random.permutation(third_key, SEC_TOK)
        return table[row_order]
    section_keys = jax.random.split(jax.random.fold_in(key, 12), sections)
    return jax.vmap(one_section)(section_keys).reshape(TOKEN_TOTAL, TOPK).astype(jnp.int32)


def raised(values, stream_key, source, target, shards_of, factor):
    owner, partner = [(jnp.arange(values.shape[axis_at]) // (values.shape[axis_at] // shards_of)).reshape([-1 if axis == axis_at else 1 for axis in range(values.ndim)]) for axis_at in (source, target)]
    chosen = jax.random.permutation(stream_key, shards_of)[partner]
    strong = (owner == chosen) | (owner == (partner + shards_of // 2) % shards_of)
    return jnp.where(strong, factor * values, values)


def steps_of(rng, extent, pieces, low, top_value):
    loudness, own = 1.0, jax.random.fold_in(rng, 6)
    for dim, shards_of in pieces:
        draws = jnp.exp(jax.random.uniform(jax.random.fold_in(own, dim), (shards_of,), jnp.float32, low / len(pieces), top_value / len(pieces)))
        loudness = loudness * jnp.repeat(draws, extent[dim] // shards_of).reshape([-1 if axis == dim else 1 for axis in range(len(extent))])
    return loudness


def gaussian(own_key, extent, spread, limit, shards=(), held_as=jnp.bfloat16):
    factor_of = steps_of(own_key, extent, shards, -0.22, 0.18) if shards else 1.0
    array = jax.random.normal(own_key, extent, jnp.float32) * spread * factor_of
    return jnp.minimum(jnp.maximum(array, -limit), limit).astype(held_as)


def bell_draw_with(stream_key, extent, spread, limit, shards, heavy, kind=jnp.bfloat16):
    drawn = spread * jax.random.normal(stream_key, extent, jnp.float32)
    if shards:
        drawn = drawn * steps_of(stream_key, extent, shards, -0.22, 0.18)
    return jnp.clip(raised(drawn, jax.random.fold_in(stream_key, 3), *heavy), -limit, limit).astype(kind)


def setup_inputs(seed: int = 0) -> dict:
    key_list = jax.random.split(jax.random.key(seed), 12)
    return {
        "attn_query": gaussian(key_list[0], (TOKEN_TOTAL, D), 1.0, 6.0, ((0, 8), (1, 16))),
        "attn_key": gaussian(key_list[1], (TOKEN_TOTAL, D), 1.0, 6.0, ((0, 8), (1, 16))),
        "attn_value": draw_attn_value(jax.random.fold_in(key_list[11], 71), 0),
        "log_decay": draw_log_decay(jax.random.fold_in(key_list[11], 71), 0),
        "residual": gaussian(key_list[4], (TOKEN_TOTAL, D), 1.0, 6.0, ((0, 8), (1, 16))),
        "norm_gain": jnp.clip(1.0 + 0.18 * jax.random.normal(key_list[5], (D,), jnp.float32), 0.099609375, 1.8984375).astype(jnp.bfloat16),
        "expert_ids": draw_expert_ids(jax.random.fold_in(key_list[11], 71), 0),
        "router_weight": gaussian(key_list[7], (D, EXPERTS), D ** -0.5, 0.078125, ((1, 8),)),
        "gate_weight": gaussian(key_list[8], (EXPERTS, D, FF), D ** -0.5, 0.078125, ((0, 8), (2, 16))),
        "up_weight": gaussian(key_list[9], (EXPERTS, D, FF), D ** -0.5, 0.078125, ((0, 8), (2, 16))),
        "down_weight": bell_draw_with(key_list[10], (EXPERTS, FF, D), FF ** -0.5, 0.125, ((0, 8), (1, 16)), (1, 2, 16, 2.0)),
    }


def section_pass(query_rows, key_rows, value_rows, decay_rows, carry_state):
    cumulative = jnp.cumsum(decay_rows, axis=1)
    length = decay_rows.shape[1]
    causal = jnp.arange(length, dtype=jnp.int32)[:, None] >= jnp.arange(length, dtype=jnp.int32)[None, :]
    decay_gap = jnp.where(causal[None], cumulative[:, :, None] - cumulative[:, None, :], 0.0)
    decay_mask = jnp.where(causal[None], jnp.exp(decay_gap), 0.0)
    scores = jnp.einsum('htd,hsd->hts', query_rows.astype(jnp.float32), key_rows.astype(jnp.float32))
    weights = (scores * decay_mask).astype(jnp.bfloat16)
    intra_part = jnp.einsum('hts,hsd->htd', weights.astype(jnp.float32), value_rows.astype(jnp.float32))
    inter_part = jnp.einsum('htd,hde->hte', query_rows.astype(jnp.float32), carry_state, precision=lax.Precision.HIGHEST)
    attn_out = intra_part + jnp.exp(cumulative)[:, :, None] * inter_part
    key_fade = jnp.exp(cumulative[:, -1:] - cumulative)
    scaled = (key_fade[:, :, None] * key_rows.astype(jnp.float32)).astype(jnp.bfloat16)
    local_state = jnp.einsum('hsd,hse->hde', scaled.astype(jnp.float32), value_rows.astype(jnp.float32))
    next_state = jnp.exp(cumulative[:, -1])[:, None, None] * carry_state + local_state
    return (attn_out, next_state)

def run_expert(expert_parts):
    input_rows, gate_matrix, up_matrix, down_matrix, router_column = expert_parts
    gate_acc = jnp.dot(input_rows, gate_matrix, preferred_element_type=jnp.float32)
    upward = jnp.dot(input_rows, up_matrix, preferred_element_type=jnp.float32)
    hidden_act = (jax.nn.silu(gate_acc) * upward).astype(jnp.bfloat16)
    expert_out = jnp.dot(hidden_act, down_matrix, preferred_element_type=jnp.float32)
    score_rows = jnp.dot(input_rows, router_column, preferred_element_type=jnp.float32)
    return (jax.nn.sigmoid(score_rows)[:, None] * expert_out).astype(jnp.bfloat16)

def reference(attn_query, attn_key, attn_value, log_decay, residual, norm_gain, expert_ids, router_weight, gate_weight, up_weight, down_weight):
    sections = TOKEN_TOTAL // SEC_TOK

    def split_heads(array_rows):
        return array_rows.reshape(sections, SEC_TOK, H, DH).transpose(0, 2, 1, 3)
    query_blocks = split_heads(attn_query)
    key_blocks = split_heads(attn_key)
    value_blocks = split_heads(attn_value)
    decay_blocks = log_decay.reshape(H, sections, SEC_TOK).transpose(1, 0, 2)

    def one_section(carry_state, section_parts):
        section_out, carry_state = section_pass(section_parts[0], section_parts[1], section_parts[2], section_parts[3], carry_state)
        return (carry_state, section_out)
    initial = jnp.zeros((H, DH, DH), jnp.float32)
    _, attn_blocks = lax.scan(one_section, initial, (query_blocks, key_blocks, value_blocks, decay_blocks))
    mean_square = lax.optimization_barrier(jnp.mean(attn_blocks * attn_blocks, axis=-1, keepdims=True))
    normed = attn_blocks / jnp.sqrt(mean_square + 1e-06)
    normed = normed.transpose(0, 2, 1, 3).reshape(TOKEN_TOTAL, D)
    stream = (residual.astype(jnp.float32) + norm_gain.astype(jnp.float32) * normed).astype(jnp.bfloat16)
    entries = expert_ids.reshape(sections, SEC_TOK * TOPK)
    onehot = (entries[:, :, None] == jnp.arange(EXPERTS, dtype=jnp.int32)[None, None, :]).astype(jnp.int32)
    running = jnp.cumsum(onehot, axis=1)
    slot_index = lax.optimization_barrier(jnp.sum(running * onehot, axis=2)) - 1
    row_index = (jnp.arange(sections, dtype=jnp.int32)[:, None] * CAP + slot_index).astype(jnp.int32)
    token_index = jnp.repeat(jnp.arange(TOKEN_TOTAL, dtype=jnp.int32).reshape(sections, SEC_TOK), TOPK, axis=1)
    flat_expert = entries.reshape(-1).astype(jnp.int32)
    flat_row = row_index.reshape(-1).astype(jnp.int32)
    buffer = jnp.zeros((EXPERTS, sections * CAP, D), jnp.bfloat16)
    buffer = buffer.at[flat_expert, flat_row].set(stream[token_index.reshape(-1)])
    routed_all = lax.map(run_expert, (buffer, gate_weight, up_weight, down_weight, router_weight.T))
    picked = routed_all[flat_expert, flat_row].reshape(TOKEN_TOTAL, TOPK, D).astype(jnp.float32)
    return (stream.astype(jnp.float32) + lax.optimization_barrier(jnp.sum(picked, axis=1))).astype(jnp.bfloat16)
```

```python
import functools

import jax
import jax.numpy as jnp
from jax import lax
from jax.sharding import PartitionSpec as P
from jax.experimental import pallas as pl
from jax.experimental.pallas import tpu as pltpu


def shifted(array, axis, by):
    count = lax.axis_size(axis)
    pairs = [(i, i + by) for i in range(count) if 0 <= i + by < count]
    return lax.ppermute(array, axis, pairs)


def down_kernel(blocks_per_step, block_width, h_ref, w_ref, o_ref):
    sections, capacity, hidden = h_ref.shape
    rows = h_ref[...].reshape(sections * capacity, hidden)
    product = jnp.dot(rows, w_ref[...], preferred_element_type=jnp.float32)
    for i in range(blocks_per_step):
        piece = product[:, i * block_width : (i + 1) * block_width]
        o_ref[i] = piece.astype(o_ref.dtype).reshape(sections, capacity, block_width)


def down_projection(hidden_act, down_weight, shards):
    sections, experts_here, capacity, hidden = hidden_act.shape
    features = down_weight.shape[2]
    block_width = features // shards
    blocks_per_step = 4
    steps = shards // blocks_per_step
    return pl.pallas_call(
        functools.partial(down_kernel, blocks_per_step, block_width),
        out_shape=jax.ShapeDtypeStruct(
            (shards, sections, experts_here, capacity, block_width), jnp.bfloat16
        ),
        grid=(experts_here, steps),
        in_specs=[
            pl.BlockSpec((sections, None, capacity, hidden), lambda j, b: (0, j, 0, 0)),
            pl.BlockSpec((None, hidden, blocks_per_step * block_width), lambda j, b: (j, 0, b)),
        ],
        out_specs=pl.BlockSpec(
            (blocks_per_step, sections, None, capacity, block_width),
            lambda j, b: (b, 0, j, 0, 0),
        ),
        cost_estimate=pl.CostEstimate(
            flops=2 * sections * experts_here * capacity * hidden * features,
            bytes_accessed=2 * (hidden_act.size + down_weight.size + hidden_act.size // hidden * features),
            transcendentals=0,
        ),
    )(hidden_act, down_weight)


def on_device(
    attn_query,
    attn_key,
    attn_value,
    log_decay,
    residual,
    norm_gain,
    expert_ids,
    router_weight,
    gate_weight,
    up_weight,
    down_weight,
):
    heads_here = log_decay.shape[0]
    length = log_decay.shape[1]
    head_size = attn_query.shape[1] // heads_here
    query_rows = attn_query.reshape(length, heads_here, head_size)
    key_rows = attn_key.reshape(length, heads_here, head_size)
    value_rows = attn_value.reshape(length, heads_here, head_size)
    cumulative = jnp.cumsum(log_decay, axis=1)
    causal = lax.broadcasted_iota(jnp.int32, (length, length), 0) >= lax.broadcasted_iota(
        jnp.int32, (length, length), 1
    )
    decay_gap = jnp.where(causal[None], cumulative[:, :, None] - cumulative[:, None, :], 0.0)
    decay_mask = jnp.where(causal[None], jnp.exp(decay_gap), 0.0)
    scores = jnp.einsum("thd,shd->hts", query_rows, key_rows, preferred_element_type=jnp.float32)
    weights = (scores * decay_mask).astype(jnp.bfloat16)
    intra_part = jnp.einsum("hts,shd->thd", weights, value_rows, preferred_element_type=jnp.float32)
    key_fade = jnp.exp(cumulative[:, -1:] - cumulative)
    scaled = (key_fade.T[:, :, None] * key_rows.astype(jnp.float32)).astype(jnp.bfloat16)
    local_state = jnp.einsum("shd,she->hde", scaled, value_rows, preferred_element_type=jnp.float32)
    section_log_fade = cumulative[:, -1]
    sections_total = lax.axis_size("seq")
    packed = jnp.concatenate(
        [local_state, jnp.broadcast_to(section_log_fade[:, None, None], (heads_here, 8, head_size))],
        axis=1,
    )
    gathered = lax.all_gather(packed, "seq", axis=0)
    all_states = gathered[:, :, :head_size, :]
    all_log_fades = gathered[:, :, head_size, 0]
    me = lax.axis_index("seq")
    section_iota = lax.broadcasted_iota(jnp.int32, (sections_total, sections_total), 0)
    between_iota = lax.broadcasted_iota(jnp.int32, (sections_total, sections_total), 1)
    between = (between_iota > section_iota) & (between_iota < me)
    log_weight = jnp.sum(
        jnp.where(between[:, :, None], all_log_fades[None, :, :], 0.0), axis=1
    )
    state_weight = jnp.where(
        lax.broadcasted_iota(jnp.int32, (sections_total, 1), 0) < me, jnp.exp(log_weight), 0.0
    )
    incoming = jnp.sum(state_weight[:, :, None, None] * all_states, axis=0)
    inter_part = jnp.einsum(
        "thd,hde->the", query_rows.astype(jnp.float32), incoming, precision=lax.Precision.HIGHEST
    )
    attn_out = intra_part + jnp.exp(cumulative).T[:, :, None] * inter_part
    mean_square = jnp.mean(attn_out * attn_out, axis=2, keepdims=True)
    normed = (attn_out / jnp.sqrt(mean_square + 1e-06)).reshape(length, heads_here * head_size)
    stream = (residual.astype(jnp.float32) + norm_gain.astype(jnp.float32) * normed).astype(
        jnp.bfloat16
    )
    experts_here = router_weight.shape[1]
    groups = lax.axis_size("seq")
    expert_count = experts_here * groups
    capacity = 4 * length // expert_count
    features = stream.shape[1]
    choices_per_token = expert_ids.shape[1]
    flat_ids = expert_ids.reshape(-1)
    expert_iota = lax.broadcasted_iota(jnp.int32, (1, expert_count), 1)
    onehot = (flat_ids[:, None] == expert_iota).astype(jnp.int32)
    running = jnp.cumsum(onehot, axis=0)
    slot_index = jnp.sum(running * onehot, axis=1) - 1
    target = flat_ids * capacity + slot_index
    place_iota = lax.broadcasted_iota(jnp.int32, (expert_count * capacity, 1), 0)
    route_matrix = (
        (place_iota == target[None, :])
        .astype(jnp.bfloat16)
        .reshape(expert_count * capacity, length, choices_per_token)
        .sum(axis=2)
    )
    outgoing = jnp.dot(route_matrix, stream, preferred_element_type=jnp.float32).astype(
        jnp.bfloat16
    )
    outgoing = outgoing.reshape(groups, experts_here, capacity, features)
    portion = lax.all_gather(
        lax.all_to_all(outgoing, "seq", split_axis=0, concat_axis=0, tiled=True),
        "exp",
        axis=3,
        tiled=True,
    )
    gate_acc = jnp.einsum(
        "sjcd,jdf->sjcf", portion, gate_weight, preferred_element_type=jnp.float32
    )
    upward = jnp.einsum("sjcd,jdf->sjcf", portion, up_weight, preferred_element_type=jnp.float32)
    logits = jnp.einsum("sjcd,dj->sjc", portion, router_weight, preferred_element_type=jnp.float32)
    hidden_act = (jax.nn.silu(gate_acc) * upward).astype(jnp.bfloat16)
    shards = lax.axis_size("exp")
    expert_out = lax.psum_scatter(
        down_projection(hidden_act, down_weight, shards),
        "exp",
        scatter_dimension=0,
        tiled=True,
    )[0].astype(jnp.float32)
    routed = (jax.nn.sigmoid(logits)[..., None] * expert_out).astype(jnp.bfloat16)
    returned = lax.all_to_all(routed, "seq", split_axis=0, concat_axis=0, tiled=True)
    returned = returned.reshape(expert_count * capacity, features)
    combined = lax.dot_general(
        route_matrix, returned, (((0,), (0,)), ((), ())), preferred_element_type=jnp.float32
    )
    return (stream.astype(jnp.float32) + combined).astype(jnp.bfloat16)


def solution(mesh):
    in_specs = (
        P("seq", "exp"),
        P("seq", "exp"),
        P("seq", "exp"),
        P("exp", "seq"),
        P("seq", "exp"),
        P("exp"),
        P("seq", None),
        P(None, "seq"),
        P("seq", None, "exp"),
        P("seq", None, "exp"),
        P("seq", "exp", None),
    )
    out_specs = P("seq", "exp")
    return jax.shard_map(
        on_device, mesh=mesh, in_specs=in_specs, out_specs=out_specs, check_vma=False
    )
```

```python
import functools

import jax
import jax.numpy as jnp
from jax import lax
from jax.sharding import PartitionSpec as P
from jax.experimental import pallas as pl
from jax.experimental.pallas import tpu as pltpu


def shifted(array, axis, by):
    count = lax.axis_size(axis)
    pairs = [(i, i + by) for i in range(count) if 0 <= i + by < count]
    return lax.ppermute(array, axis, pairs)


def down_kernel(blocks_per_step, block_width, h_ref, w_ref, o_ref):
    sections, capacity, hidden = h_ref.shape
    rows = h_ref[...].reshape(sections * capacity, hidden)
    product = jnp.dot(rows, w_ref[...], preferred_element_type=jnp.float32)
    for i in range(blocks_per_step):
        piece = product[:, i * block_width : (i + 1) * block_width]
        o_ref[i] = piece.astype(o_ref.dtype).reshape(sections, capacity, block_width)


def down_projection(hidden_act, down_weight, shards):
    sections, experts_here, capacity, hidden = hidden_act.shape
    features = down_weight.shape[2]
    block_width = features // shards
    blocks_per_step = 4
    steps = shards // blocks_per_step
    return pl.pallas_call(
        functools.partial(down_kernel, blocks_per_step, block_width),
        out_shape=jax.ShapeDtypeStruct(
            (shards, sections, experts_here, capacity, block_width), jnp.bfloat16
        ),
        grid=(experts_here, steps),
        in_specs=[
            pl.BlockSpec((sections, None, capacity, hidden), lambda j, b: (0, j, 0, 0)),
            pl.BlockSpec((None, hidden, blocks_per_step * block_width), lambda j, b: (j, 0, b)),
        ],
        out_specs=pl.BlockSpec(
            (blocks_per_step, sections, None, capacity, block_width),
            lambda j, b: (b, 0, j, 0, 0),
        ),
        cost_estimate=pl.CostEstimate(
            flops=2 * sections * experts_here * capacity * hidden * features,
            bytes_accessed=2 * (hidden_act.size + down_weight.size + hidden_act.size // hidden * features),
            transcendentals=0,
        ),
    )(hidden_act, down_weight)


def on_device(
    attn_query,
    attn_key,
    attn_value,
    log_decay,
    residual,
    norm_gain,
    expert_ids,
    router_weight,
    gate_weight,
    up_weight,
    down_weight,
):
    heads_here = log_decay.shape[0]
    length = log_decay.shape[1]
    head_size = attn_query.shape[1] // heads_here
    query_rows = attn_query.reshape(length, heads_here, head_size)
    key_rows = attn_key.reshape(length, heads_here, head_size)
    value_rows = attn_value.reshape(length, heads_here, head_size)
    cumulative = jnp.cumsum(log_decay, axis=1)
    causal = lax.broadcasted_iota(jnp.int32, (length, length), 0) >= lax.broadcasted_iota(
        jnp.int32, (length, length), 1
    )
    decay_gap = jnp.where(causal[None], cumulative[:, :, None] - cumulative[:, None, :], 0.0)
    decay_mask = jnp.where(causal[None], jnp.exp(decay_gap), 0.0)
    scores = jnp.einsum("thd,shd->hts", query_rows, key_rows, preferred_element_type=jnp.float32)
    weights = (scores * decay_mask).astype(jnp.bfloat16)
    intra_part = jnp.einsum("hts,shd->thd", weights, value_rows, preferred_element_type=jnp.float32)
    key_fade = jnp.exp(cumulative[:, -1:] - cumulative)
    scaled = (key_fade.T[:, :, None] * key_rows.astype(jnp.float32)).astype(jnp.bfloat16)
    local_state = jnp.einsum("shd,she->hde", scaled, value_rows, preferred_element_type=jnp.float32)
    section_log_fade = cumulative[:, -1]
    sections_total = lax.axis_size("seq")
    packed = jnp.concatenate(
        [local_state, jnp.broadcast_to(section_log_fade[:, None, None], (heads_here, 8, head_size))],
        axis=1,
    )
    gathered = lax.all_gather(packed, "seq", axis=0)
    all_states = gathered[:, :, :head_size, :]
    all_log_fades = gathered[:, :, head_size, 0]
    me = lax.axis_index("seq")
    section_iota = lax.broadcasted_iota(jnp.int32, (sections_total, sections_total), 0)
    between_iota = lax.broadcasted_iota(jnp.int32, (sections_total, sections_total), 1)
    between = (between_iota > section_iota) & (between_iota < me)
    log_weight = jnp.sum(
        jnp.where(between[:, :, None], all_log_fades[None, :, :], 0.0), axis=1
    )
    state_weight = jnp.where(
        lax.broadcasted_iota(jnp.int32, (sections_total, 1), 0) < me, jnp.exp(log_weight), 0.0
    )
    incoming = jnp.sum(state_weight[:, :, None, None] * all_states, axis=0)
    inter_part = jnp.einsum(
        "thd,hde->the", query_rows.astype(jnp.float32), incoming, precision=lax.Precision.HIGHEST
    )
    attn_out = intra_part + jnp.exp(cumulative).T[:, :, None] * inter_part
    mean_square = jnp.mean(attn_out * attn_out, axis=2, keepdims=True)
    normed = (attn_out / jnp.sqrt(mean_square + 1e-06)).reshape(length, heads_here * head_size)
    stream = (residual.astype(jnp.float32) + norm_gain.astype(jnp.float32) * normed).astype(
        jnp.bfloat16
    )
    experts_here = router_weight.shape[1]
    groups = lax.axis_size("seq")
    expert_count = experts_here * groups
    capacity = 4 * length // expert_count
    features = stream.shape[1]
    choices_per_token = expert_ids.shape[1]
    flat_ids = expert_ids.reshape(-1)
    expert_iota = lax.broadcasted_iota(jnp.int32, (1, expert_count), 1)
    onehot = (flat_ids[:, None] == expert_iota).astype(jnp.int32)
    running = jnp.cumsum(onehot, axis=0)
    slot_index = jnp.sum(running * onehot, axis=1) - 1
    target = flat_ids * capacity + slot_index
    place_iota = lax.broadcasted_iota(jnp.int32, (expert_count * capacity, 1), 0)
    route_matrix = (
        (place_iota == target[None, :])
        .astype(jnp.bfloat16)
        .reshape(expert_count * capacity, length, choices_per_token)
        .sum(axis=2)
    )
    shards = lax.axis_size("exp")
    route_blocks = route_matrix.reshape(groups, experts_here, capacity, length)
    combined = jnp.zeros((length, features), jnp.float32)
    for j in range(experts_here):
        route_j = route_blocks[:, j].reshape(groups * capacity, length)
        outgoing = jnp.dot(route_j, stream, preferred_element_type=jnp.float32).astype(
            jnp.bfloat16
        )
        outgoing = outgoing.reshape(groups, capacity, features)
        portion = lax.all_gather(
            lax.all_to_all(outgoing, "seq", split_axis=0, concat_axis=0, tiled=True),
            "exp",
            axis=2,
            tiled=True,
        )
        gate_acc = jnp.einsum(
            "scd,df->scf", portion, gate_weight[j], preferred_element_type=jnp.float32
        )
        upward = jnp.einsum(
            "scd,df->scf", portion, up_weight[j], preferred_element_type=jnp.float32
        )
        logits = jnp.einsum(
            "scd,d->sc", portion, router_weight[:, j], preferred_element_type=jnp.float32
        )
        hidden_act = (jax.nn.silu(gate_acc) * upward).astype(jnp.bfloat16)
        expert_out = lax.psum_scatter(
            down_projection(hidden_act[:, None], down_weight[j : j + 1], shards),
            "exp",
            scatter_dimension=0,
            tiled=True,
        )[0, :, 0].astype(jnp.float32)
        routed = (jax.nn.sigmoid(logits)[..., None] * expert_out).astype(jnp.bfloat16)
        returned = lax.all_to_all(routed, "seq", split_axis=0, concat_axis=0, tiled=True)
        returned = returned.reshape(groups * capacity, features)
        combined = combined + lax.dot_general(
            route_j, returned, (((0,), (0,)), ((), ())), preferred_element_type=jnp.float32
        )
    return (stream.astype(jnp.float32) + combined).astype(jnp.bfloat16)


def solution(mesh):
    in_specs = (
        P("seq", "exp"),
        P("seq", "exp"),
        P("seq", "exp"),
        P("exp", "seq"),
        P("seq", "exp"),
        P("exp"),
        P("seq", None),
        P(None, "seq"),
        P("seq", None, "exp"),
        P("seq", None, "exp"),
        P("seq", "exp", None),
    )
    out_specs = P("seq", "exp")
    return jax.shard_map(
        on_device, mesh=mesh, in_specs=in_specs, out_specs=out_specs, check_vma=False
    )
```

```python
import functools

import jax
import jax.numpy as jnp
from jax import lax
from jax.sharding import PartitionSpec as P
from jax.experimental import pallas as pl
from jax.experimental.pallas import tpu as pltpu


def shifted(array, axis, by):
    count = lax.axis_size(axis)
    pairs = [(i, i + by) for i in range(count) if 0 <= i + by < count]
    return lax.ppermute(array, axis, pairs)


def down_kernel(blocks_per_step, block_width, h_ref, w_ref, o_ref):
    sections, capacity, hidden = h_ref.shape
    rows = h_ref[...].reshape(sections * capacity, hidden)
    product = jnp.dot(rows, w_ref[...], preferred_element_type=jnp.float32)
    for i in range(blocks_per_step):
        piece = product[:, i * block_width : (i + 1) * block_width]
        o_ref[i] = piece.astype(o_ref.dtype).reshape(sections, capacity, block_width)


def down_projection(hidden_act, down_weight, shards):
    sections, experts_here, capacity, hidden = hidden_act.shape
    features = down_weight.shape[2]
    block_width = features // shards
    blocks_per_step = 4
    steps = shards // blocks_per_step
    return pl.pallas_call(
        functools.partial(down_kernel, blocks_per_step, block_width),
        out_shape=jax.ShapeDtypeStruct(
            (shards, sections, experts_here, capacity, block_width), jnp.bfloat16
        ),
        grid=(experts_here, steps),
        in_specs=[
            pl.BlockSpec((sections, None, capacity, hidden), lambda j, b: (0, j, 0, 0)),
            pl.BlockSpec((None, hidden, blocks_per_step * block_width), lambda j, b: (j, 0, b)),
        ],
        out_specs=pl.BlockSpec(
            (blocks_per_step, sections, None, capacity, block_width),
            lambda j, b: (b, 0, j, 0, 0),
        ),
        cost_estimate=pl.CostEstimate(
            flops=2 * sections * experts_here * capacity * hidden * features,
            bytes_accessed=2 * (hidden_act.size + down_weight.size + hidden_act.size // hidden * features),
            transcendentals=0,
        ),
    )(hidden_act, down_weight)


def on_device(
    attn_query,
    attn_key,
    attn_value,
    log_decay,
    residual,
    norm_gain,
    expert_ids,
    router_weight,
    gate_weight,
    up_weight,
    down_weight,
):
    heads_here = log_decay.shape[0]
    length = log_decay.shape[1]
    head_size = attn_query.shape[1] // heads_here
    query_rows = attn_query.reshape(length, heads_here, head_size)
    key_rows = attn_key.reshape(length, heads_here, head_size)
    value_rows = attn_value.reshape(length, heads_here, head_size)
    cumulative = jnp.cumsum(log_decay, axis=1)
    causal = lax.broadcasted_iota(jnp.int32, (length, length), 0) >= lax.broadcasted_iota(
        jnp.int32, (length, length), 1
    )
    decay_gap = jnp.where(causal[None], cumulative[:, :, None] - cumulative[:, None, :], 0.0)
    decay_mask = jnp.where(causal[None], jnp.exp(decay_gap), 0.0)
    scores = jnp.einsum("thd,shd->hts", query_rows, key_rows, preferred_element_type=jnp.float32)
    weights = (scores * decay_mask).astype(jnp.bfloat16)
    intra_part = jnp.einsum("hts,shd->thd", weights, value_rows, preferred_element_type=jnp.float32)
    key_fade = jnp.exp(cumulative[:, -1:] - cumulative)
    scaled = (key_fade.T[:, :, None] * key_rows.astype(jnp.float32)).astype(jnp.bfloat16)
    local_state = jnp.einsum("shd,she->hde", scaled, value_rows, preferred_element_type=jnp.float32)
    section_log_fade = cumulative[:, -1]
    sections_total = lax.axis_size("seq")
    packed = jnp.concatenate(
        [local_state, jnp.broadcast_to(section_log_fade[:, None, None], (heads_here, 8, head_size))],
        axis=1,
    )
    gathered = lax.all_gather(packed, "seq", axis=0)
    all_states = gathered[:, :, :head_size, :]
    all_log_fades = gathered[:, :, head_size, 0]
    me = lax.axis_index("seq")
    section_iota = lax.broadcasted_iota(jnp.int32, (sections_total, sections_total), 0)
    between_iota = lax.broadcasted_iota(jnp.int32, (sections_total, sections_total), 1)
    between = (between_iota > section_iota) & (between_iota < me)
    log_weight = jnp.sum(
        jnp.where(between[:, :, None], all_log_fades[None, :, :], 0.0), axis=1
    )
    state_weight = jnp.where(
        lax.broadcasted_iota(jnp.int32, (sections_total, 1), 0) < me, jnp.exp(log_weight), 0.0
    )
    incoming = jnp.sum(state_weight[:, :, None, None] * all_states, axis=0)
    inter_part = jnp.einsum(
        "thd,hde->the", query_rows.astype(jnp.float32), incoming, precision=lax.Precision.HIGHEST
    )
    attn_out = intra_part + jnp.exp(cumulative).T[:, :, None] * inter_part
    mean_square = jnp.mean(attn_out * attn_out, axis=2, keepdims=True)
    normed = (attn_out / jnp.sqrt(mean_square + 1e-06)).reshape(length, heads_here * head_size)
    stream = (residual.astype(jnp.float32) + norm_gain.astype(jnp.float32) * normed).astype(
        jnp.bfloat16
    )
    experts_here = router_weight.shape[1]
    groups = lax.axis_size("seq")
    expert_count = experts_here * groups
    capacity = 4 * length // expert_count
    features = stream.shape[1]
    choices_per_token = expert_ids.shape[1]
    flat_ids = expert_ids.reshape(-1)
    expert_iota = lax.broadcasted_iota(jnp.int32, (1, expert_count), 1)
    onehot = (flat_ids[:, None] == expert_iota).astype(jnp.int32)
    running = jnp.cumsum(onehot, axis=0)
    slot_index = jnp.sum(running * onehot, axis=1) - 1
    target = flat_ids * capacity + slot_index
    place_iota = lax.broadcasted_iota(jnp.int32, (expert_count * capacity, 1), 0)
    route_matrix = (
        (place_iota == target[None, :])
        .astype(jnp.bfloat16)
        .reshape(expert_count * capacity, length, choices_per_token)
        .sum(axis=2)
    )
    outgoing = jnp.dot(route_matrix, stream, preferred_element_type=jnp.float32).astype(
        jnp.bfloat16
    )
    outgoing = outgoing.reshape(groups, experts_here, capacity, features)
    shards = lax.axis_size("exp")
    portion = lax.all_gather(
        lax.all_to_all(outgoing, "seq", split_axis=0, concat_axis=0, tiled=True),
        "exp",
        axis=0,
    )
    hidden_units = gate_weight.shape[2]
    gate_blocks = gate_weight.reshape(experts_here, shards, features, hidden_units)
    up_blocks = up_weight.reshape(experts_here, shards, features, hidden_units)
    router_blocks = router_weight.reshape(shards, features, experts_here)
    gate_acc = jnp.einsum(
        "esjcd,jedf->sjcf", portion, gate_blocks, preferred_element_type=jnp.float32
    )
    upward = jnp.einsum(
        "esjcd,jedf->sjcf", portion, up_blocks, preferred_element_type=jnp.float32
    )
    logits = jnp.einsum(
        "esjcd,edj->sjc", portion, router_blocks, preferred_element_type=jnp.float32
    )
    hidden_act = (jax.nn.silu(gate_acc) * upward).astype(jnp.bfloat16)
    expert_out = lax.psum_scatter(
        down_projection(hidden_act, down_weight, shards),
        "exp",
        scatter_dimension=0,
        tiled=True,
    )[0].astype(jnp.float32)
    routed = (jax.nn.sigmoid(logits)[..., None] * expert_out).astype(jnp.bfloat16)
    returned = lax.all_to_all(routed, "seq", split_axis=0, concat_axis=0, tiled=True)
    returned = returned.reshape(expert_count * capacity, features)
    combined = lax.dot_general(
        route_matrix, returned, (((0,), (0,)), ((), ())), preferred_element_type=jnp.float32
    )
    return (stream.astype(jnp.float32) + combined).astype(jnp.bfloat16)


def solution(mesh):
    in_specs = (
        P("seq", "exp"),
        P("seq", "exp"),
        P("seq", "exp"),
        P("exp", "seq"),
        P("seq", "exp"),
        P("exp"),
        P("seq", None),
        P(None, "seq"),
        P("seq", None, "exp"),
        P("seq", None, "exp"),
        P("seq", "exp", None),
    )
    out_specs = P("seq", "exp")
    return jax.shard_map(
        on_device, mesh=mesh, in_specs=in_specs, out_specs=out_specs, check_vma=False
    )
```

```python
import functools

import jax
import jax.numpy as jnp
from jax import lax
from jax.sharding import PartitionSpec as P
from jax.experimental import pallas as pl
from jax.experimental.pallas import tpu as pltpu


def shifted(array, axis, by):
    count = lax.axis_size(axis)
    pairs = [(i, i + by) for i in range(count) if 0 <= i + by < count]
    return lax.ppermute(array, axis, pairs)


def down_kernel(blocks_per_step, block_width, h_ref, w_ref, o_ref):
    sections, capacity, hidden = h_ref.shape
    rows = h_ref[...].reshape(sections * capacity, hidden)
    product = jnp.dot(rows, w_ref[...], preferred_element_type=jnp.float32)
    for i in range(blocks_per_step):
        piece = product[:, i * block_width : (i + 1) * block_width]
        o_ref[i] = piece.astype(o_ref.dtype).reshape(sections, capacity, block_width)


def down_projection(hidden_act, down_weight, shards):
    sections, experts_here, capacity, hidden = hidden_act.shape
    features = down_weight.shape[2]
    block_width = features // shards
    blocks_per_step = 4
    steps = shards // blocks_per_step
    return pl.pallas_call(
        functools.partial(down_kernel, blocks_per_step, block_width),
        out_shape=jax.ShapeDtypeStruct(
            (shards, sections, experts_here, capacity, block_width), jnp.bfloat16
        ),
        grid=(experts_here, steps),
        in_specs=[
            pl.BlockSpec((sections, None, capacity, hidden), lambda j, b: (0, j, 0, 0)),
            pl.BlockSpec((None, hidden, blocks_per_step * block_width), lambda j, b: (j, 0, b)),
        ],
        out_specs=pl.BlockSpec(
            (blocks_per_step, sections, None, capacity, block_width),
            lambda j, b: (b, 0, j, 0, 0),
        ),
        cost_estimate=pl.CostEstimate(
            flops=2 * sections * experts_here * capacity * hidden * features,
            bytes_accessed=2 * (hidden_act.size + down_weight.size + hidden_act.size // hidden * features),
            transcendentals=0,
        ),
    )(hidden_act, down_weight)


def exchange_kernel(x_ref, o_ref, send_sem, recv_sem, local_sem):
    n = x_ref.shape[0]
    me = lax.axis_index("seq")
    col = lax.axis_index("exp")
    mesh_id = pl.DeviceIdType.MESH
    barrier = pltpu.get_barrier_semaphore()
    for k in range(1, n):
        peer = lax.rem(me + k, n)
        pl.semaphore_signal(barrier, inc=1, device_id=(peer, col), device_id_type=mesh_id)
    pl.semaphore_wait(barrier, n - 1)
    local = pltpu.make_async_copy(x_ref.at[me], o_ref.at[me], local_sem)
    local.start()
    copies = []
    for k in range(1, n):
        peer = lax.rem(me + k, n)
        copy = pltpu.make_async_remote_copy(
            src_ref=x_ref.at[peer],
            dst_ref=o_ref.at[me],
            send_sem=send_sem.at[k],
            recv_sem=recv_sem.at[k],
            device_id=(peer, col),
            device_id_type=mesh_id,
        )
        copy.start()
        copies.append(copy)
    local.wait()
    for copy in copies:
        copy.wait()


def exchange(x, collective_id):
    n = x.shape[0]
    return pl.pallas_call(
        exchange_kernel,
        out_shape=jax.ShapeDtypeStruct(x.shape, x.dtype),
        in_specs=[pl.BlockSpec(memory_space=pltpu.VMEM)],
        out_specs=pl.BlockSpec(memory_space=pltpu.VMEM),
        scratch_shapes=[
            pltpu.SemaphoreType.DMA((n,)),
            pltpu.SemaphoreType.DMA((n,)),
            pltpu.SemaphoreType.DMA,
        ],
        compiler_params=pltpu.CompilerParams(collective_id=collective_id, has_side_effects=True),
    )(x)


def on_device(
    attn_query,
    attn_key,
    attn_value,
    log_decay,
    residual,
    norm_gain,
    expert_ids,
    router_weight,
    gate_weight,
    up_weight,
    down_weight,
):
    heads_here = log_decay.shape[0]
    length = log_decay.shape[1]
    head_size = attn_query.shape[1] // heads_here
    query_rows = attn_query.reshape(length, heads_here, head_size)
    key_rows = attn_key.reshape(length, heads_here, head_size)
    value_rows = attn_value.reshape(length, heads_here, head_size)
    cumulative = jnp.cumsum(log_decay, axis=1)
    causal = lax.broadcasted_iota(jnp.int32, (length, length), 0) >= lax.broadcasted_iota(
        jnp.int32, (length, length), 1
    )
    decay_gap = jnp.where(causal[None], cumulative[:, :, None] - cumulative[:, None, :], 0.0)
    decay_mask = jnp.where(causal[None], jnp.exp(decay_gap), 0.0)
    scores = jnp.einsum("thd,shd->hts", query_rows, key_rows, preferred_element_type=jnp.float32)
    weights = (scores * decay_mask).astype(jnp.bfloat16)
    intra_part = jnp.einsum("hts,shd->thd", weights, value_rows, preferred_element_type=jnp.float32)
    key_fade = jnp.exp(cumulative[:, -1:] - cumulative)
    scaled = (key_fade.T[:, :, None] * key_rows.astype(jnp.float32)).astype(jnp.bfloat16)
    local_state = jnp.einsum("shd,she->hde", scaled, value_rows, preferred_element_type=jnp.float32)
    section_log_fade = cumulative[:, -1]
    sections_total = lax.axis_size("seq")
    packed = jnp.concatenate(
        [local_state, jnp.broadcast_to(section_log_fade[:, None, None], (heads_here, 8, head_size))],
        axis=1,
    )
    gathered = lax.all_gather(packed, "seq", axis=0)
    all_states = gathered[:, :, :head_size, :]
    all_log_fades = gathered[:, :, head_size, 0]
    me = lax.axis_index("seq")
    section_iota = lax.broadcasted_iota(jnp.int32, (sections_total, sections_total), 0)
    between_iota = lax.broadcasted_iota(jnp.int32, (sections_total, sections_total), 1)
    between = (between_iota > section_iota) & (between_iota < me)
    log_weight = jnp.sum(
        jnp.where(between[:, :, None], all_log_fades[None, :, :], 0.0), axis=1
    )
    state_weight = jnp.where(
        lax.broadcasted_iota(jnp.int32, (sections_total, 1), 0) < me, jnp.exp(log_weight), 0.0
    )
    incoming = jnp.sum(state_weight[:, :, None, None] * all_states, axis=0)
    inter_part = jnp.einsum(
        "thd,hde->the", query_rows.astype(jnp.float32), incoming, precision=lax.Precision.HIGHEST
    )
    attn_out = intra_part + jnp.exp(cumulative).T[:, :, None] * inter_part
    mean_square = jnp.mean(attn_out * attn_out, axis=2, keepdims=True)
    normed = (attn_out / jnp.sqrt(mean_square + 1e-06)).reshape(length, heads_here * head_size)
    stream = (residual.astype(jnp.float32) + norm_gain.astype(jnp.float32) * normed).astype(
        jnp.bfloat16
    )
    experts_here = router_weight.shape[1]
    groups = lax.axis_size("seq")
    expert_count = experts_here * groups
    capacity = 4 * length // expert_count
    features = stream.shape[1]
    choices_per_token = expert_ids.shape[1]
    flat_ids = expert_ids.reshape(-1)
    expert_iota = lax.broadcasted_iota(jnp.int32, (1, expert_count), 1)
    onehot = (flat_ids[:, None] == expert_iota).astype(jnp.int32)
    running = jnp.cumsum(onehot, axis=0)
    slot_index = jnp.sum(running * onehot, axis=1) - 1
    target = flat_ids * capacity + slot_index
    place_iota = lax.broadcasted_iota(jnp.int32, (expert_count * capacity, 1), 0)
    route_matrix = (
        (place_iota == target[None, :])
        .astype(jnp.bfloat16)
        .reshape(expert_count * capacity, length, choices_per_token)
        .sum(axis=2)
    )
    outgoing = jnp.dot(route_matrix, stream, preferred_element_type=jnp.float32).astype(
        jnp.bfloat16
    )
    outgoing = outgoing.reshape(groups, experts_here, capacity, features)
    shards = lax.axis_size("exp")
    portion = lax.all_gather(
        exchange(outgoing, 0),
        "exp",
        axis=0,
    )
    hidden_units = gate_weight.shape[2]
    gate_blocks = gate_weight.reshape(experts_here, shards, features, hidden_units)
    up_blocks = up_weight.reshape(experts_here, shards, features, hidden_units)
    router_blocks = router_weight.reshape(shards, features, experts_here)
    gate_acc = jnp.einsum(
        "esjcd,jedf->sjcf", portion, gate_blocks, preferred_element_type=jnp.float32
    )
    upward = jnp.einsum(
        "esjcd,jedf->sjcf", portion, up_blocks, preferred_element_type=jnp.float32
    )
    logits = jnp.einsum(
        "esjcd,edj->sjc", portion, router_blocks, preferred_element_type=jnp.float32
    )
    hidden_act = (jax.nn.silu(gate_acc) * upward).astype(jnp.bfloat16)
    expert_out = lax.psum_scatter(
        down_projection(hidden_act, down_weight, shards),
        "exp",
        scatter_dimension=0,
        tiled=True,
    )[0].astype(jnp.float32)
    routed = (jax.nn.sigmoid(logits)[..., None] * expert_out).astype(jnp.bfloat16)
    returned = exchange(routed, 1)
    returned = returned.reshape(expert_count * capacity, features)
    combined = lax.dot_general(
        route_matrix, returned, (((0,), (0,)), ((), ())), preferred_element_type=jnp.float32
    )
    return (stream.astype(jnp.float32) + combined).astype(jnp.bfloat16)


def solution(mesh):
    in_specs = (
        P("seq", "exp"),
        P("seq", "exp"),
        P("seq", "exp"),
        P("exp", "seq"),
        P("seq", "exp"),
        P("exp"),
        P("seq", None),
        P(None, "seq"),
        P("seq", None, "exp"),
        P("seq", None, "exp"),
        P("seq", "exp", None),
    )
    out_specs = P("seq", "exp")
    return jax.shard_map(
        on_device, mesh=mesh, in_specs=in_specs, out_specs=out_specs, check_vma=False
    )
```

```python
import functools

import jax
import jax.numpy as jnp
from jax import lax
from jax.sharding import PartitionSpec as P
from jax.experimental import pallas as pl
from jax.experimental.pallas import tpu as pltpu


def shifted(array, axis, by):
    count = lax.axis_size(axis)
    pairs = [(i, i + by) for i in range(count) if 0 <= i + by < count]
    return lax.ppermute(array, axis, pairs)


def down_kernel(blocks_per_step, block_width, h_ref, w_ref, o_ref):
    sections, capacity, hidden = h_ref.shape
    rows = h_ref[...].reshape(sections * capacity, hidden)
    product = jnp.dot(rows, w_ref[...], preferred_element_type=jnp.float32)
    for i in range(blocks_per_step):
        piece = product[:, i * block_width : (i + 1) * block_width]
        o_ref[i] = piece.astype(o_ref.dtype).reshape(sections, capacity, block_width)


def down_projection(hidden_act, down_weight, shards):
    sections, experts_here, capacity, hidden = hidden_act.shape
    features = down_weight.shape[2]
    block_width = features // shards
    blocks_per_step = 8
    steps = shards // blocks_per_step
    return pl.pallas_call(
        functools.partial(down_kernel, blocks_per_step, block_width),
        out_shape=jax.ShapeDtypeStruct(
            (shards, sections, experts_here, capacity, block_width), jnp.bfloat16
        ),
        grid=(experts_here, steps),
        in_specs=[
            pl.BlockSpec((sections, None, capacity, hidden), lambda j, b: (0, j, 0, 0)),
            pl.BlockSpec((None, hidden, blocks_per_step * block_width), lambda j, b: (j, 0, b)),
        ],
        out_specs=pl.BlockSpec(
            (blocks_per_step, sections, None, capacity, block_width),
            lambda j, b: (b, 0, j, 0, 0),
        ),
        cost_estimate=pl.CostEstimate(
            flops=2 * sections * experts_here * capacity * hidden * features,
            bytes_accessed=2 * (hidden_act.size + down_weight.size + hidden_act.size // hidden * features),
            transcendentals=0,
        ),
    )(hidden_act, down_weight)


def exchange_kernel(x_ref, o_ref, send_sem, recv_sem, local_sem):
    n = x_ref.shape[0]
    me = lax.axis_index("seq")
    col = lax.axis_index("exp")
    mesh_id = pl.DeviceIdType.MESH
    barrier = pltpu.get_barrier_semaphore()
    for k in range(1, n):
        peer = lax.rem(me + k, n)
        pl.semaphore_signal(barrier, inc=1, device_id=(peer, col), device_id_type=mesh_id)
    pl.semaphore_wait(barrier, n - 1)
    local = pltpu.make_async_copy(x_ref.at[me], o_ref.at[me], local_sem)
    local.start()
    copies = []
    for k in range(1, n):
        peer = lax.rem(me + k, n)
        copy = pltpu.make_async_remote_copy(
            src_ref=x_ref.at[peer],
            dst_ref=o_ref.at[me],
            send_sem=send_sem.at[k],
            recv_sem=recv_sem.at[k],
            device_id=(peer, col),
            device_id_type=mesh_id,
        )
        copy.start()
        copies.append(copy)
    local.wait()
    for copy in copies:
        copy.wait()


def exchange(x, collective_id):
    n = x.shape[0]
    return pl.pallas_call(
        exchange_kernel,
        out_shape=jax.ShapeDtypeStruct(x.shape, x.dtype),
        in_specs=[pl.BlockSpec(memory_space=pltpu.VMEM)],
        out_specs=pl.BlockSpec(memory_space=pltpu.VMEM),
        scratch_shapes=[
            pltpu.SemaphoreType.DMA((n,)),
            pltpu.SemaphoreType.DMA((n,)),
            pltpu.SemaphoreType.DMA,
        ],
        compiler_params=pltpu.CompilerParams(collective_id=collective_id, has_side_effects=True),
    )(x)


def on_device(
    attn_query,
    attn_key,
    attn_value,
    log_decay,
    residual,
    norm_gain,
    expert_ids,
    router_weight,
    gate_weight,
    up_weight,
    down_weight,
):
    heads_here = log_decay.shape[0]
    length = log_decay.shape[1]
    head_size = attn_query.shape[1] // heads_here
    query_rows = attn_query.reshape(length, heads_here, head_size)
    key_rows = attn_key.reshape(length, heads_here, head_size)
    value_rows = attn_value.reshape(length, heads_here, head_size)
    cumulative = jnp.cumsum(log_decay, axis=1)
    causal = lax.broadcasted_iota(jnp.int32, (length, length), 0) >= lax.broadcasted_iota(
        jnp.int32, (length, length), 1
    )
    decay_gap = jnp.where(causal[None], cumulative[:, :, None] - cumulative[:, None, :], 0.0)
    decay_mask = jnp.where(causal[None], jnp.exp(decay_gap), 0.0)
    scores = jnp.einsum("thd,shd->hts", query_rows, key_rows, preferred_element_type=jnp.float32)
    weights = (scores * decay_mask).astype(jnp.bfloat16)
    intra_part = jnp.einsum("hts,shd->thd", weights, value_rows, preferred_element_type=jnp.float32)
    key_fade = jnp.exp(cumulative[:, -1:] - cumulative)
    scaled = (key_fade.T[:, :, None] * key_rows.astype(jnp.float32)).astype(jnp.bfloat16)
    local_state = jnp.einsum("shd,she->hde", scaled, value_rows, preferred_element_type=jnp.float32)
    section_log_fade = cumulative[:, -1]
    sections_total = lax.axis_size("seq")
    packed = jnp.concatenate(
        [local_state, jnp.broadcast_to(section_log_fade[:, None, None], (heads_here, 8, head_size))],
        axis=1,
    )
    gathered = lax.all_gather(packed, "seq", axis=0)
    all_states = gathered[:, :, :head_size, :]
    all_log_fades = gathered[:, :, head_size, 0]
    me = lax.axis_index("seq")
    section_iota = lax.broadcasted_iota(jnp.int32, (sections_total, sections_total), 0)
    between_iota = lax.broadcasted_iota(jnp.int32, (sections_total, sections_total), 1)
    between = (between_iota > section_iota) & (between_iota < me)
    log_weight = jnp.sum(
        jnp.where(between[:, :, None], all_log_fades[None, :, :], 0.0), axis=1
    )
    state_weight = jnp.where(
        lax.broadcasted_iota(jnp.int32, (sections_total, 1), 0) < me, jnp.exp(log_weight), 0.0
    )
    incoming = jnp.sum(state_weight[:, :, None, None] * all_states, axis=0)
    inter_part = jnp.einsum(
        "thd,hde->the", query_rows.astype(jnp.float32), incoming, precision=lax.Precision.HIGHEST
    )
    attn_out = intra_part + jnp.exp(cumulative).T[:, :, None] * inter_part
    mean_square = jnp.mean(attn_out * attn_out, axis=2, keepdims=True)
    normed = (attn_out / jnp.sqrt(mean_square + 1e-06)).reshape(length, heads_here * head_size)
    stream = (residual.astype(jnp.float32) + norm_gain.astype(jnp.float32) * normed).astype(
        jnp.bfloat16
    )
    experts_here = router_weight.shape[1]
    groups = lax.axis_size("seq")
    expert_count = experts_here * groups
    capacity = 4 * length // expert_count
    features = stream.shape[1]
    choices_per_token = expert_ids.shape[1]
    flat_ids = expert_ids.reshape(-1)
    expert_iota = lax.broadcasted_iota(jnp.int32, (1, expert_count), 1)
    onehot = (flat_ids[:, None] == expert_iota).astype(jnp.int32)
    running = jnp.cumsum(onehot, axis=0)
    slot_index = jnp.sum(running * onehot, axis=1) - 1
    target = flat_ids * capacity + slot_index
    place_iota = lax.broadcasted_iota(jnp.int32, (expert_count * capacity, 1), 0)
    route_matrix = (
        (place_iota == target[None, :])
        .astype(jnp.bfloat16)
        .reshape(expert_count * capacity, length, choices_per_token)
        .sum(axis=2)
    )
    outgoing = jnp.dot(route_matrix, stream, preferred_element_type=jnp.float32).astype(
        jnp.bfloat16
    )
    outgoing = outgoing.reshape(groups, experts_here, capacity, features)
    shards = lax.axis_size("exp")
    portion = lax.all_gather(
        exchange(outgoing, 0),
        "exp",
        axis=0,
    )
    hidden_units = gate_weight.shape[2]
    gate_blocks = gate_weight.reshape(experts_here, shards, features, hidden_units)
    up_blocks = up_weight.reshape(experts_here, shards, features, hidden_units)
    router_blocks = router_weight.reshape(shards, features, experts_here)
    gate_up = jnp.einsum(
        "esjcd,jedf->sjcf",
        portion,
        jnp.concatenate([gate_blocks, up_blocks], axis=3),
        preferred_element_type=jnp.float32,
    )
    gate_acc = gate_up[..., :hidden_units]
    upward = gate_up[..., hidden_units:]
    logits = jnp.einsum(
        "esjcd,edj->sjc", portion, router_blocks, preferred_element_type=jnp.float32
    )
    hidden_act = (jax.nn.silu(gate_acc) * upward).astype(jnp.bfloat16)
    expert_out = lax.psum_scatter(
        down_projection(hidden_act, down_weight, shards),
        "exp",
        scatter_dimension=0,
        tiled=True,
    )[0].astype(jnp.float32)
    routed = (jax.nn.sigmoid(logits)[..., None] * expert_out).astype(jnp.bfloat16)
    returned = exchange(routed, 1)
    returned = returned.reshape(expert_count * capacity, features)
    combined = lax.dot_general(
        route_matrix, returned, (((0,), (0,)), ((), ())), preferred_element_type=jnp.float32
    )
    return (stream.astype(jnp.float32) + combined).astype(jnp.bfloat16)


def solution(mesh):
    in_specs = (
        P("seq", "exp"),
        P("seq", "exp"),
        P("seq", "exp"),
        P("exp", "seq"),
        P("seq", "exp"),
        P("exp"),
        P("seq", None),
        P(None, "seq"),
        P("seq", None, "exp"),
        P("seq", None, "exp"),
        P("seq", "exp", None),
    )
    out_specs = P("seq", "exp")
    return jax.shard_map(
        on_device, mesh=mesh, in_specs=in_specs, out_specs=out_specs, check_vma=False
    )
```

```python
import functools

import jax
import jax.numpy as jnp
from jax import lax
from jax.sharding import PartitionSpec as P
from jax.experimental import pallas as pl
from jax.experimental.pallas import tpu as pltpu


def shifted(array, axis, by):
    count = lax.axis_size(axis)
    pairs = [(i, i + by) for i in range(count) if 0 <= i + by < count]
    return lax.ppermute(array, axis, pairs)


def down_kernel(blocks_per_step, block_width, h_ref, w_ref, o_ref):
    sections, capacity, hidden = h_ref.shape
    rows = h_ref[...].reshape(sections * capacity, hidden)
    product = jnp.dot(rows, w_ref[...], preferred_element_type=jnp.float32)
    for i in range(blocks_per_step):
        piece = product[:, i * block_width : (i + 1) * block_width]
        o_ref[i] = piece.astype(o_ref.dtype).reshape(sections, capacity, block_width)


def down_projection(hidden_act, down_weight, shards):
    sections, experts_here, capacity, hidden = hidden_act.shape
    features = down_weight.shape[2]
    block_width = features // shards
    blocks_per_step = 8
    steps = shards // blocks_per_step
    return pl.pallas_call(
        functools.partial(down_kernel, blocks_per_step, block_width),
        out_shape=jax.ShapeDtypeStruct(
            (shards, sections, experts_here, capacity, block_width), jnp.bfloat16
        ),
        grid=(experts_here, steps),
        in_specs=[
            pl.BlockSpec((sections, None, capacity, hidden), lambda j, b: (0, j, 0, 0)),
            pl.BlockSpec((None, hidden, blocks_per_step * block_width), lambda j, b: (j, 0, b)),
        ],
        out_specs=pl.BlockSpec(
            (blocks_per_step, sections, None, capacity, block_width),
            lambda j, b: (b, 0, j, 0, 0),
        ),
        cost_estimate=pl.CostEstimate(
            flops=2 * sections * experts_here * capacity * hidden * features,
            bytes_accessed=2 * (hidden_act.size + down_weight.size + hidden_act.size // hidden * features),
            transcendentals=0,
        ),
    )(hidden_act, down_weight)


def exchange_kernel(x_ref, o_ref, send_sem, recv_sem, local_sem):
    n = x_ref.shape[0]
    me = lax.axis_index("seq")
    col = lax.axis_index("exp")
    mesh_id = pl.DeviceIdType.MESH
    barrier = pltpu.get_barrier_semaphore()
    for k in range(1, n):
        peer = lax.rem(me + k, n)
        pl.semaphore_signal(barrier, inc=1, device_id=(peer, col), device_id_type=mesh_id)
    pl.semaphore_wait(barrier, n - 1)
    local = pltpu.make_async_copy(x_ref.at[me], o_ref.at[me], local_sem)
    local.start()
    copies = []
    for k in range(1, n):
        peer = lax.rem(me + k, n)
        copy = pltpu.make_async_remote_copy(
            src_ref=x_ref.at[peer],
            dst_ref=o_ref.at[me],
            send_sem=send_sem.at[k],
            recv_sem=recv_sem.at[k],
            device_id=(peer, col),
            device_id_type=mesh_id,
        )
        copy.start()
        copies.append(copy)
    local.wait()
    for copy in copies:
        copy.wait()


def exchange(x, collective_id):
    n = x.shape[0]
    return pl.pallas_call(
        exchange_kernel,
        out_shape=jax.ShapeDtypeStruct(x.shape, x.dtype),
        in_specs=[pl.BlockSpec(memory_space=pltpu.VMEM)],
        out_specs=pl.BlockSpec(memory_space=pltpu.VMEM),
        scratch_shapes=[
            pltpu.SemaphoreType.DMA((n,)),
            pltpu.SemaphoreType.DMA((n,)),
            pltpu.SemaphoreType.DMA,
        ],
        compiler_params=pltpu.CompilerParams(collective_id=collective_id, has_side_effects=True),
    )(x)


def scan_kernel(x_ref, o_ref, state, received, send_sem, recv_sem):
    n = lax.axis_size("seq")
    me = lax.axis_index("seq")
    col = lax.axis_index("exp")
    mesh_id = pl.DeviceIdType.MESH
    size = x_ref.shape[1] - 8
    barrier = pltpu.get_barrier_semaphore()
    for k in range(1, n):
        peer = lax.rem(me + k, n)
        pl.semaphore_signal(barrier, inc=1, device_id=(peer, col), device_id_type=mesh_id)
    pl.semaphore_wait(barrier, n - 1)
    shifts = [1, 1, 2, 4]
    for r, d in enumerate(shifts):
        source = x_ref if r == 0 else state.at[r - 1]
        copy = pltpu.make_async_remote_copy(
            src_ref=source,
            dst_ref=received.at[r],
            send_sem=send_sem.at[r],
            recv_sem=recv_sem.at[r],
            device_id=(lax.rem(me + d, n), col),
            device_id_type=mesh_id,
        )
        copy.start()
        copy.wait()
        has_input = me - d >= 0
        other = received[r]
        if r == 0:
            row = lax.broadcasted_iota(jnp.int32, other.shape, 1)
            identity = jnp.where(row < size, 0.0, 1.0).astype(jnp.float32)
            state[r] = jnp.where(has_input, other, identity)
        else:
            mine = state[r - 1]
            fade = mine[:, size : size + 1, :]
            combined_state = fade * other[:, :size, :] + mine[:, :size, :]
            combined_fade = mine[:, size:, :] * other[:, size:, :]
            state[r, :, :size, :] = jnp.where(has_input, combined_state, mine[:, :size, :])
            state[r, :, size:, :] = jnp.where(has_input, combined_fade, mine[:, size:, :])

    o_ref[...] = state[len(shifts) - 1, :, :size, :]


def incoming_state(packed):
    heads, rows, width = packed.shape
    steps = 4
    return pl.pallas_call(
        scan_kernel,
        out_shape=jax.ShapeDtypeStruct((heads, rows - 8, width), jnp.float32),
        in_specs=[pl.BlockSpec(memory_space=pltpu.VMEM)],
        out_specs=pl.BlockSpec(memory_space=pltpu.VMEM),
        scratch_shapes=[
            pltpu.VMEM((steps, heads, rows, width), jnp.float32),
            pltpu.VMEM((steps, heads, rows, width), jnp.float32),
            pltpu.SemaphoreType.DMA((steps,)),
            pltpu.SemaphoreType.DMA((steps,)),
        ],
        compiler_params=pltpu.CompilerParams(collective_id=2, has_side_effects=True),
    )(packed)


def on_device(
    attn_query,
    attn_key,
    attn_value,
    log_decay,
    residual,
    norm_gain,
    expert_ids,
    router_weight,
    gate_weight,
    up_weight,
    down_weight,
):
    heads_here = log_decay.shape[0]
    length = log_decay.shape[1]
    head_size = attn_query.shape[1] // heads_here
    query_rows = attn_query.reshape(length, heads_here, head_size)
    key_rows = attn_key.reshape(length, heads_here, head_size)
    value_rows = attn_value.reshape(length, heads_here, head_size)
    cumulative = jnp.cumsum(log_decay, axis=1)
    causal = lax.broadcasted_iota(jnp.int32, (length, length), 0) >= lax.broadcasted_iota(
        jnp.int32, (length, length), 1
    )
    decay_gap = jnp.where(causal[None], cumulative[:, :, None] - cumulative[:, None, :], 0.0)
    decay_mask = jnp.where(causal[None], jnp.exp(decay_gap), 0.0)
    scores = jnp.einsum("thd,shd->hts", query_rows, key_rows, preferred_element_type=jnp.float32)
    weights = (scores * decay_mask).astype(jnp.bfloat16)
    intra_part = jnp.einsum("hts,shd->thd", weights, value_rows, preferred_element_type=jnp.float32)
    key_fade = jnp.exp(cumulative[:, -1:] - cumulative)
    scaled = (key_fade.T[:, :, None] * key_rows.astype(jnp.float32)).astype(jnp.bfloat16)
    local_state = jnp.einsum("shd,she->hde", scaled, value_rows, preferred_element_type=jnp.float32)
    section_fade = jnp.exp(cumulative[:, -1])
    packed = jnp.concatenate(
        [local_state, jnp.broadcast_to(section_fade[:, None, None], (heads_here, 8, head_size))],
        axis=1,
    )
    incoming = incoming_state(packed)
    inter_part = jnp.einsum(
        "thd,hde->the", query_rows.astype(jnp.float32), incoming, precision=lax.Precision.HIGHEST
    )
    attn_out = intra_part + jnp.exp(cumulative).T[:, :, None] * inter_part
    mean_square = jnp.mean(attn_out * attn_out, axis=2, keepdims=True)
    normed = (attn_out / jnp.sqrt(mean_square + 1e-06)).reshape(length, heads_here * head_size)
    stream = (residual.astype(jnp.float32) + norm_gain.astype(jnp.float32) * normed).astype(
        jnp.bfloat16
    )
    experts_here = router_weight.shape[1]
    groups = lax.axis_size("seq")
    expert_count = experts_here * groups
    capacity = 4 * length // expert_count
    features = stream.shape[1]
    choices_per_token = expert_ids.shape[1]
    flat_ids = expert_ids.reshape(-1)
    expert_iota = lax.broadcasted_iota(jnp.int32, (1, expert_count), 1)
    onehot = (flat_ids[:, None] == expert_iota).astype(jnp.int32)
    running = jnp.cumsum(onehot, axis=0)
    slot_index = jnp.sum(running * onehot, axis=1) - 1
    target = flat_ids * capacity + slot_index
    place_iota = lax.broadcasted_iota(jnp.int32, (expert_count * capacity, 1), 0)
    route_matrix = (
        (place_iota == target[None, :])
        .astype(jnp.bfloat16)
        .reshape(expert_count * capacity, length, choices_per_token)
        .sum(axis=2)
    )
    outgoing = jnp.dot(route_matrix, stream, preferred_element_type=jnp.float32).astype(
        jnp.bfloat16
    )
    outgoing = outgoing.reshape(groups, experts_here, capacity, features)
    shards = lax.axis_size("exp")
    portion = lax.all_gather(
        exchange(outgoing, 0),
        "exp",
        axis=0,
    )
    hidden_units = gate_weight.shape[2]
    gate_blocks = gate_weight.reshape(experts_here, shards, features, hidden_units)
    up_blocks = up_weight.reshape(experts_here, shards, features, hidden_units)
    router_blocks = router_weight.reshape(shards, features, experts_here)
    gate_up = jnp.einsum(
        "esjcd,jedf->sjcf",
        portion,
        jnp.concatenate([gate_blocks, up_blocks], axis=3),
        preferred_element_type=jnp.float32,
    )
    gate_acc = gate_up[..., :hidden_units]
    upward = gate_up[..., hidden_units:]
    logits = jnp.einsum(
        "esjcd,edj->sjc", portion, router_blocks, preferred_element_type=jnp.float32
    )
    hidden_act = (jax.nn.silu(gate_acc) * upward).astype(jnp.bfloat16)
    expert_out = lax.psum_scatter(
        down_projection(hidden_act, down_weight, shards),
        "exp",
        scatter_dimension=0,
        tiled=True,
    )[0].astype(jnp.float32)
    routed = (jax.nn.sigmoid(logits)[..., None] * expert_out).astype(jnp.bfloat16)
    returned = exchange(routed, 1)
    returned = returned.reshape(expert_count * capacity, features)
    combined = lax.dot_general(
        route_matrix, returned, (((0,), (0,)), ((), ())), preferred_element_type=jnp.float32
    )
    return (stream.astype(jnp.float32) + combined).astype(jnp.bfloat16)


def solution(mesh):
    in_specs = (
        P("seq", "exp"),
        P("seq", "exp"),
        P("seq", "exp"),
        P("exp", "seq"),
        P("seq", "exp"),
        P("exp"),
        P("seq", None),
        P(None, "seq"),
        P("seq", None, "exp"),
        P("seq", None, "exp"),
        P("seq", "exp", None),
    )
    out_specs = P("seq", "exp")
    return jax.shard_map(
        on_device, mesh=mesh, in_specs=in_specs, out_specs=out_specs, check_vma=False
    )
```

```python
import functools

import jax
import jax.numpy as jnp
from jax import lax
from jax.sharding import PartitionSpec as P
from jax.experimental import pallas as pl
from jax.experimental.pallas import tpu as pltpu


def shifted(array, axis, by):
    count = lax.axis_size(axis)
    pairs = [(i, i + by) for i in range(count) if 0 <= i + by < count]
    return lax.ppermute(array, axis, pairs)


def down_kernel(blocks_per_step, block_width, h_ref, w_ref, o_ref):
    sections, capacity, hidden = h_ref.shape
    rows = h_ref[...].reshape(sections * capacity, hidden)
    product = jnp.dot(rows, w_ref[...], preferred_element_type=jnp.float32)
    for i in range(blocks_per_step):
        piece = product[:, i * block_width : (i + 1) * block_width]
        o_ref[i] = piece.astype(o_ref.dtype).reshape(sections, capacity, block_width)


def down_projection(hidden_act, down_weight, shards):
    sections, experts_here, capacity, hidden = hidden_act.shape
    features = down_weight.shape[2]
    block_width = features // shards
    blocks_per_step = 8
    steps = shards // blocks_per_step
    return pl.pallas_call(
        functools.partial(down_kernel, blocks_per_step, block_width),
        out_shape=jax.ShapeDtypeStruct(
            (shards, sections, experts_here, capacity, block_width), jnp.bfloat16
        ),
        grid=(experts_here, steps),
        in_specs=[
            pl.BlockSpec((sections, None, capacity, hidden), lambda j, b: (0, j, 0, 0)),
            pl.BlockSpec((None, hidden, blocks_per_step * block_width), lambda j, b: (j, 0, b)),
        ],
        out_specs=pl.BlockSpec(
            (blocks_per_step, sections, None, capacity, block_width),
            lambda j, b: (b, 0, j, 0, 0),
        ),
        cost_estimate=pl.CostEstimate(
            flops=2 * sections * experts_here * capacity * hidden * features,
            bytes_accessed=2 * (hidden_act.size + down_weight.size + hidden_act.size // hidden * features),
            transcendentals=0,
        ),
    )(hidden_act, down_weight)


def exchange_kernel(x_ref, o_ref, send_sem, recv_sem, local_sem):
    n = x_ref.shape[0]
    me = lax.axis_index("seq")
    col = lax.axis_index("exp")
    mesh_id = pl.DeviceIdType.MESH
    barrier = pltpu.get_barrier_semaphore()
    for k in range(1, n):
        peer = lax.rem(me + k, n)
        pl.semaphore_signal(barrier, inc=1, device_id=(peer, col), device_id_type=mesh_id)
    pl.semaphore_wait(barrier, n - 1)
    local = pltpu.make_async_copy(x_ref.at[me], o_ref.at[me], local_sem)
    local.start()
    copies = []
    for k in range(1, n):
        peer = lax.rem(me + k, n)
        copy = pltpu.make_async_remote_copy(
            src_ref=x_ref.at[peer],
            dst_ref=o_ref.at[me],
            send_sem=send_sem.at[k],
            recv_sem=recv_sem.at[k],
            device_id=(peer, col),
            device_id_type=mesh_id,
        )
        copy.start()
        copies.append(copy)
    local.wait()
    for copy in copies:
        copy.wait()


def exchange(x, collective_id):
    n = x.shape[0]
    return pl.pallas_call(
        exchange_kernel,
        out_shape=jax.ShapeDtypeStruct(x.shape, x.dtype),
        in_specs=[pl.BlockSpec(memory_space=pltpu.VMEM)],
        out_specs=pl.BlockSpec(memory_space=pltpu.VMEM),
        scratch_shapes=[
            pltpu.SemaphoreType.DMA((n,)),
            pltpu.SemaphoreType.DMA((n,)),
            pltpu.SemaphoreType.DMA,
        ],
        compiler_params=pltpu.CompilerParams(collective_id=collective_id, has_side_effects=True),
    )(x)


def scan_kernel(x_ref, o_ref, state, received, send_sem, recv_sem):
    n = lax.axis_size("seq")
    me = lax.axis_index("seq")
    col = lax.axis_index("exp")
    mesh_id = pl.DeviceIdType.MESH
    size = x_ref.shape[1] - 8
    barrier = pltpu.get_barrier_semaphore()
    for k in range(1, n):
        peer = lax.rem(me + k, n)
        pl.semaphore_signal(barrier, inc=1, device_id=(peer, col), device_id_type=mesh_id)
    pl.semaphore_wait(barrier, n - 1)
    row = lax.broadcasted_iota(jnp.int32, x_ref.shape, 1)
    identity = jnp.where(row < size, 0.0, 1.0).astype(jnp.float32)

    def compose(later, earlier):
        fade = later[:, size : size + 1, :]
        return jnp.concatenate(
            [
                fade * earlier[:, :size, :] + later[:, :size, :],
                later[:, size:, :] * earlier[:, size:, :],
            ],
            axis=1,
        )

    def send(source, slot, d):
        copy = pltpu.make_async_remote_copy(
            src_ref=source,
            dst_ref=received.at[slot],
            send_sem=send_sem.at[slot],
            recv_sem=recv_sem.at[slot],
            device_id=(lax.rem(me + d, n), col),
            device_id_type=mesh_id,
        )
        copy.start()
        return copy

    def arrived(slot, d):
        return jnp.where(me - d >= 0, received[slot], identity)

    first = send(x_ref, 0, 1)
    second = send(x_ref, 1, 2)
    first.wait()
    second.wait()
    state[0] = compose(arrived(0, 1), arrived(1, 2))
    shifts = [2, 4]
    for r, d in enumerate(shifts):
        copy = send(state.at[r], r + 2, d)
        copy.wait()
        state[r + 1] = compose(state[r], arrived(r + 2, d))

    o_ref[...] = state[len(shifts), :, :size, :]


def incoming_state(packed):
    heads, rows, width = packed.shape
    steps = 4
    return pl.pallas_call(
        scan_kernel,
        out_shape=jax.ShapeDtypeStruct((heads, rows - 8, width), jnp.float32),
        in_specs=[pl.BlockSpec(memory_space=pltpu.VMEM)],
        out_specs=pl.BlockSpec(memory_space=pltpu.VMEM),
        scratch_shapes=[
            pltpu.VMEM((steps, heads, rows, width), jnp.float32),
            pltpu.VMEM((steps, heads, rows, width), jnp.float32),
            pltpu.SemaphoreType.DMA((steps,)),
            pltpu.SemaphoreType.DMA((steps,)),
        ],
        compiler_params=pltpu.CompilerParams(collective_id=2, has_side_effects=True),
    )(packed)


def on_device(
    attn_query,
    attn_key,
    attn_value,
    log_decay,
    residual,
    norm_gain,
    expert_ids,
    router_weight,
    gate_weight,
    up_weight,
    down_weight,
):
    heads_here = log_decay.shape[0]
    length = log_decay.shape[1]
    head_size = attn_query.shape[1] // heads_here
    query_rows = attn_query.reshape(length, heads_here, head_size)
    key_rows = attn_key.reshape(length, heads_here, head_size)
    value_rows = attn_value.reshape(length, heads_here, head_size)
    cumulative = jnp.cumsum(log_decay, axis=1)
    causal = lax.broadcasted_iota(jnp.int32, (length, length), 0) >= lax.broadcasted_iota(
        jnp.int32, (length, length), 1
    )
    decay_gap = jnp.where(causal[None], cumulative[:, :, None] - cumulative[:, None, :], 0.0)
    decay_mask = jnp.where(causal[None], jnp.exp(decay_gap), 0.0)
    scores = jnp.einsum("thd,shd->hts", query_rows, key_rows, preferred_element_type=jnp.float32)
    weights = (scores * decay_mask).astype(jnp.bfloat16)
    intra_part = jnp.einsum("hts,shd->thd", weights, value_rows, preferred_element_type=jnp.float32)
    key_fade = jnp.exp(cumulative[:, -1:] - cumulative)
    scaled = (key_fade.T[:, :, None] * key_rows.astype(jnp.float32)).astype(jnp.bfloat16)
    local_state = jnp.einsum("shd,she->hde", scaled, value_rows, preferred_element_type=jnp.float32)
    section_fade = jnp.exp(cumulative[:, -1])
    packed = jnp.concatenate(
        [local_state, jnp.broadcast_to(section_fade[:, None, None], (heads_here, 8, head_size))],
        axis=1,
    )
    incoming = incoming_state(packed)
    inter_part = jnp.einsum(
        "thd,hde->the", query_rows.astype(jnp.float32), incoming, precision=lax.Precision.HIGHEST
    )
    attn_out = intra_part + jnp.exp(cumulative).T[:, :, None] * inter_part
    mean_square = jnp.mean(attn_out * attn_out, axis=2, keepdims=True)
    normed = (attn_out / jnp.sqrt(mean_square + 1e-06)).reshape(length, heads_here * head_size)
    stream = (residual.astype(jnp.float32) + norm_gain.astype(jnp.float32) * normed).astype(
        jnp.bfloat16
    )
    experts_here = router_weight.shape[1]
    groups = lax.axis_size("seq")
    expert_count = experts_here * groups
    capacity = 4 * length // expert_count
    features = stream.shape[1]
    choices_per_token = expert_ids.shape[1]
    flat_ids = expert_ids.reshape(-1)
    expert_iota = lax.broadcasted_iota(jnp.int32, (1, expert_count), 1)
    onehot = (flat_ids[:, None] == expert_iota).astype(jnp.int32)
    running = jnp.cumsum(onehot, axis=0)
    slot_index = jnp.sum(running * onehot, axis=1) - 1
    target = flat_ids * capacity + slot_index
    place_iota = lax.broadcasted_iota(jnp.int32, (expert_count * capacity, 1), 0)
    route_matrix = (
        (place_iota == target[None, :])
        .astype(jnp.bfloat16)
        .reshape(expert_count * capacity, length, choices_per_token)
        .sum(axis=2)
    )
    outgoing = jnp.dot(route_matrix, stream, preferred_element_type=jnp.float32).astype(
        jnp.bfloat16
    )
    outgoing = outgoing.reshape(groups, experts_here, capacity, features)
    shards = lax.axis_size("exp")
    portion = lax.all_gather(
        exchange(outgoing, 0),
        "exp",
        axis=0,
    )
    hidden_units = gate_weight.shape[2]
    gate_blocks = gate_weight.reshape(experts_here, shards, features, hidden_units)
    up_blocks = up_weight.reshape(experts_here, shards, features, hidden_units)
    router_blocks = router_weight.reshape(shards, features, experts_here)
    gate_up = jnp.einsum(
        "esjcd,jedf->sjcf",
        portion,
        jnp.concatenate([gate_blocks, up_blocks], axis=3),
        preferred_element_type=jnp.float32,
    )
    gate_acc = gate_up[..., :hidden_units]
    upward = gate_up[..., hidden_units:]
    logits = jnp.einsum(
        "esjcd,edj->sjc", portion, router_blocks, preferred_element_type=jnp.float32
    )
    hidden_act = (jax.nn.silu(gate_acc) * upward).astype(jnp.bfloat16)
    expert_out = lax.psum_scatter(
        down_projection(hidden_act, down_weight, shards),
        "exp",
        scatter_dimension=0,
        tiled=True,
    )[0].astype(jnp.float32)
    routed = (jax.nn.sigmoid(logits)[..., None] * expert_out).astype(jnp.bfloat16)
    returned = exchange(routed, 1)
    returned = returned.reshape(expert_count * capacity, features)
    combined = lax.dot_general(
        route_matrix, returned, (((0,), (0,)), ((), ())), preferred_element_type=jnp.float32
    )
    return (stream.astype(jnp.float32) + combined).astype(jnp.bfloat16)


def solution(mesh):
    in_specs = (
        P("seq", "exp"),
        P("seq", "exp"),
        P("seq", "exp"),
        P("exp", "seq"),
        P("seq", "exp"),
        P("exp"),
        P("seq", None),
        P(None, "seq"),
        P("seq", None, "exp"),
        P("seq", None, "exp"),
        P("seq", "exp", None),
    )
    out_specs = P("seq", "exp")
    return jax.shard_map(
        on_device, mesh=mesh, in_specs=in_specs, out_specs=out_specs, check_vma=False
    )
```

```python
import functools

import jax
import jax.numpy as jnp
from jax import lax
from jax.sharding import PartitionSpec as P
from jax.experimental import pallas as pl
from jax.experimental.pallas import tpu as pltpu


def shifted(array, axis, by):
    count = lax.axis_size(axis)
    pairs = [(i, i + by) for i in range(count) if 0 <= i + by < count]
    return lax.ppermute(array, axis, pairs)


def down_kernel(blocks_per_step, block_width, h_ref, w_ref, o_ref):
    sections, capacity, hidden = h_ref.shape
    rows = h_ref[...].reshape(sections * capacity, hidden)
    product = jnp.dot(rows, w_ref[...], preferred_element_type=jnp.float32)
    for i in range(blocks_per_step):
        piece = product[:, i * block_width : (i + 1) * block_width]
        o_ref[i] = piece.astype(o_ref.dtype).reshape(sections, capacity, block_width)


def down_projection(hidden_act, down_weight, shards):
    sections, experts_here, capacity, hidden = hidden_act.shape
    features = down_weight.shape[2]
    block_width = features // shards
    blocks_per_step = 8
    steps = shards // blocks_per_step
    return pl.pallas_call(
        functools.partial(down_kernel, blocks_per_step, block_width),
        out_shape=jax.ShapeDtypeStruct(
            (shards, sections, experts_here, capacity, block_width), jnp.bfloat16
        ),
        grid=(experts_here, steps),
        in_specs=[
            pl.BlockSpec((sections, None, capacity, hidden), lambda j, b: (0, j, 0, 0)),
            pl.BlockSpec((None, hidden, blocks_per_step * block_width), lambda j, b: (j, 0, b)),
        ],
        out_specs=pl.BlockSpec(
            (blocks_per_step, sections, None, capacity, block_width),
            lambda j, b: (b, 0, j, 0, 0),
        ),
        cost_estimate=pl.CostEstimate(
            flops=2 * sections * experts_here * capacity * hidden * features,
            bytes_accessed=2 * (hidden_act.size + down_weight.size + hidden_act.size // hidden * features),
            transcendentals=0,
        ),
    )(hidden_act, down_weight)


def exchange_kernel(x_ref, o_ref, send_sem, recv_sem, local_sem):
    n = x_ref.shape[0]
    me = lax.axis_index("seq")
    col = lax.axis_index("exp")
    mesh_id = pl.DeviceIdType.MESH
    barrier = pltpu.get_barrier_semaphore()
    for k in range(1, n):
        peer = lax.rem(me + k, n)
        pl.semaphore_signal(barrier, inc=1, device_id=(peer, col), device_id_type=mesh_id)
    pl.semaphore_wait(barrier, n - 1)
    local = pltpu.make_async_copy(x_ref.at[me], o_ref.at[me], local_sem)
    local.start()
    copies = []
    for k in range(1, n):
        peer = lax.rem(me + k, n)
        copy = pltpu.make_async_remote_copy(
            src_ref=x_ref.at[peer],
            dst_ref=o_ref.at[me],
            send_sem=send_sem.at[k],
            recv_sem=recv_sem.at[k],
            device_id=(peer, col),
            device_id_type=mesh_id,
        )
        copy.start()
        copies.append(copy)
    local.wait()
    for copy in copies:
        copy.wait()


def exchange(x, collective_id):
    n = x.shape[0]
    return pl.pallas_call(
        exchange_kernel,
        out_shape=jax.ShapeDtypeStruct(x.shape, x.dtype),
        in_specs=[pl.BlockSpec(memory_space=pltpu.VMEM)],
        out_specs=pl.BlockSpec(memory_space=pltpu.VMEM),
        scratch_shapes=[
            pltpu.SemaphoreType.DMA((n,)),
            pltpu.SemaphoreType.DMA((n,)),
            pltpu.SemaphoreType.DMA,
        ],
        compiler_params=pltpu.CompilerParams(collective_id=collective_id, has_side_effects=True),
    )(x)


def scan_kernel(x_ref, o_ref, state, received, send_sem, recv_sem):
    n = lax.axis_size("seq")
    me = lax.axis_index("seq")
    col = lax.axis_index("exp")
    mesh_id = pl.DeviceIdType.MESH
    size = x_ref.shape[1] - 8
    barrier = pltpu.get_barrier_semaphore()
    for k in range(1, n):
        peer = lax.rem(me + k, n)
        pl.semaphore_signal(barrier, inc=1, device_id=(peer, col), device_id_type=mesh_id)
    pl.semaphore_wait(barrier, n - 1)
    shifts = [1, 1, 2, 4]
    for r, d in enumerate(shifts):
        source = x_ref if r == 0 else state.at[r - 1]
        copy = pltpu.make_async_remote_copy(
            src_ref=source,
            dst_ref=received.at[r],
            send_sem=send_sem.at[r],
            recv_sem=recv_sem.at[r],
            device_id=(lax.rem(me + d, n), col),
            device_id_type=mesh_id,
        )
        copy.start()
        copy.wait()
        has_input = me - d >= 0
        other = received[r]
        if r == 0:
            row = lax.broadcasted_iota(jnp.int32, other.shape, 1)
            identity = jnp.where(row < size, 0.0, 1.0).astype(jnp.float32)
            state[r] = jnp.where(has_input, other, identity)
        else:
            mine = state[r - 1]
            fade = mine[:, size : size + 1, :]
            combined_state = fade * other[:, :size, :] + mine[:, :size, :]
            combined_fade = mine[:, size:, :] * other[:, size:, :]
            state[r, :, :size, :] = jnp.where(has_input, combined_state, mine[:, :size, :])
            state[r, :, size:, :] = jnp.where(has_input, combined_fade, mine[:, size:, :])

    o_ref[...] = state[len(shifts) - 1, :, :size, :]


def incoming_state(packed):
    heads, rows, width = packed.shape
    steps = 4
    return pl.pallas_call(
        scan_kernel,
        out_shape=jax.ShapeDtypeStruct((heads, rows - 8, width), jnp.float32),
        in_specs=[pl.BlockSpec(memory_space=pltpu.VMEM)],
        out_specs=pl.BlockSpec(memory_space=pltpu.VMEM),
        scratch_shapes=[
            pltpu.VMEM((steps, heads, rows, width), jnp.float32),
            pltpu.VMEM((steps, heads, rows, width), jnp.float32),
            pltpu.SemaphoreType.DMA((steps,)),
            pltpu.SemaphoreType.DMA((steps,)),
        ],
        compiler_params=pltpu.CompilerParams(collective_id=2, has_side_effects=True),
    )(packed)


def on_device(
    attn_query,
    attn_key,
    attn_value,
    log_decay,
    residual,
    norm_gain,
    expert_ids,
    router_weight,
    gate_weight,
    up_weight,
    down_weight,
):
    heads_here = log_decay.shape[0]
    length = log_decay.shape[1]
    head_size = attn_query.shape[1] // heads_here
    query_rows = attn_query.reshape(length, heads_here, head_size)
    key_rows = attn_key.reshape(length, heads_here, head_size)
    value_rows = attn_value.reshape(length, heads_here, head_size)
    cumulative = jnp.cumsum(log_decay, axis=1)
    causal = lax.broadcasted_iota(jnp.int32, (length, length), 0) >= lax.broadcasted_iota(
        jnp.int32, (length, length), 1
    )
    decay_gap = jnp.where(causal[None], cumulative[:, :, None] - cumulative[:, None, :], 0.0)
    decay_mask = jnp.where(causal[None], jnp.exp(decay_gap), 0.0)
    scores = jnp.einsum("thd,shd->hts", query_rows, key_rows, preferred_element_type=jnp.float32)
    weights = (scores * decay_mask).astype(jnp.bfloat16)
    intra_part = jnp.einsum("hts,shd->thd", weights, value_rows, preferred_element_type=jnp.float32)
    key_fade = jnp.exp(cumulative[:, -1:] - cumulative)
    scaled = (key_fade.T[:, :, None] * key_rows.astype(jnp.float32)).astype(jnp.bfloat16)
    local_state = jnp.einsum("shd,she->hde", scaled, value_rows, preferred_element_type=jnp.float32)
    section_fade = jnp.exp(cumulative[:, -1])
    packed = jnp.concatenate(
        [local_state, jnp.broadcast_to(section_fade[:, None, None], (heads_here, 8, head_size))],
        axis=1,
    )
    experts_here = router_weight.shape[1]
    groups = lax.axis_size("seq")
    expert_count = experts_here * groups
    capacity = 4 * length // expert_count
    features = residual.shape[1]
    choices_per_token = expert_ids.shape[1]
    flat_ids = expert_ids.reshape(-1)
    expert_iota = lax.broadcasted_iota(jnp.int32, (1, expert_count), 1)
    onehot = (flat_ids[:, None] == expert_iota).astype(jnp.int32)
    running = jnp.cumsum(onehot, axis=0)
    slot_index = jnp.sum(running * onehot, axis=1) - 1
    target = flat_ids * capacity + slot_index
    place_iota = lax.broadcasted_iota(jnp.int32, (expert_count * capacity, 1), 0)
    route_matrix = (
        (place_iota == target[None, :])
        .astype(jnp.bfloat16)
        .reshape(expert_count * capacity, length, choices_per_token)
        .sum(axis=2)
    )
    packed, route_matrix = lax.optimization_barrier((packed, route_matrix))
    incoming = incoming_state(packed)
    inter_part = jnp.einsum(
        "thd,hde->the", query_rows.astype(jnp.float32), incoming, precision=lax.Precision.HIGHEST
    )
    attn_out = intra_part + jnp.exp(cumulative).T[:, :, None] * inter_part
    mean_square = jnp.mean(attn_out * attn_out, axis=2, keepdims=True)
    normed = (attn_out / jnp.sqrt(mean_square + 1e-06)).reshape(length, heads_here * head_size)
    stream = (residual.astype(jnp.float32) + norm_gain.astype(jnp.float32) * normed).astype(
        jnp.bfloat16
    )
    outgoing = jnp.dot(route_matrix, stream, preferred_element_type=jnp.float32).astype(
        jnp.bfloat16
    )
    outgoing = outgoing.reshape(groups, experts_here, capacity, features)
    shards = lax.axis_size("exp")
    portion = lax.all_gather(
        exchange(outgoing, 0),
        "exp",
        axis=0,
    )
    hidden_units = gate_weight.shape[2]
    gate_blocks = gate_weight.reshape(experts_here, shards, features, hidden_units)
    up_blocks = up_weight.reshape(experts_here, shards, features, hidden_units)
    router_blocks = router_weight.reshape(shards, features, experts_here)
    gate_up = jnp.einsum(
        "esjcd,jedf->sjcf",
        portion,
        jnp.concatenate([gate_blocks, up_blocks], axis=3),
        preferred_element_type=jnp.float32,
    )
    gate_acc = gate_up[..., :hidden_units]
    upward = gate_up[..., hidden_units:]
    logits = jnp.einsum(
        "esjcd,edj->sjc", portion, router_blocks, preferred_element_type=jnp.float32
    )
    hidden_act = (jax.nn.silu(gate_acc) * upward).astype(jnp.bfloat16)
    expert_out = lax.psum_scatter(
        down_projection(hidden_act, down_weight, shards),
        "exp",
        scatter_dimension=0,
        tiled=True,
    )[0].astype(jnp.float32)
    routed = (jax.nn.sigmoid(logits)[..., None] * expert_out).astype(jnp.bfloat16)
    returned = exchange(routed, 1)
    returned = returned.reshape(expert_count * capacity, features)
    combined = lax.dot_general(
        route_matrix, returned, (((0,), (0,)), ((), ())), preferred_element_type=jnp.float32
    )
    return (stream.astype(jnp.float32) + combined).astype(jnp.bfloat16)


def solution(mesh):
    in_specs = (
        P("seq", "exp"),
        P("seq", "exp"),
        P("seq", "exp"),
        P("exp", "seq"),
        P("seq", "exp"),
        P("exp"),
        P("seq", None),
        P(None, "seq"),
        P("seq", None, "exp"),
        P("seq", None, "exp"),
        P("seq", "exp", None),
    )
    out_specs = P("seq", "exp")
    return jax.shard_map(
        on_device, mesh=mesh, in_specs=in_specs, out_specs=out_specs, check_vma=False
    )
```

```python
import functools

import jax
import jax.numpy as jnp
from jax import lax
from jax.sharding import PartitionSpec as P
from jax.experimental import pallas as pl
from jax.experimental.pallas import tpu as pltpu


def shifted(array, axis, by):
    count = lax.axis_size(axis)
    pairs = [(i, i + by) for i in range(count) if 0 <= i + by < count]
    return lax.ppermute(array, axis, pairs)


def down_kernel(blocks_per_step, block_width, h_ref, w_ref, o_ref):
    sections, capacity, hidden = h_ref.shape
    rows = h_ref[...].reshape(sections * capacity, hidden)
    product = jnp.dot(rows, w_ref[...], preferred_element_type=jnp.float32)
    for i in range(blocks_per_step):
        piece = product[:, i * block_width : (i + 1) * block_width]
        o_ref[i] = piece.astype(o_ref.dtype).reshape(sections, capacity, block_width)


def down_projection(hidden_act, down_weight, shards):
    sections, experts_here, capacity, hidden = hidden_act.shape
    features = down_weight.shape[2]
    block_width = features // shards
    blocks_per_step = 8
    steps = shards // blocks_per_step
    return pl.pallas_call(
        functools.partial(down_kernel, blocks_per_step, block_width),
        out_shape=jax.ShapeDtypeStruct(
            (shards, sections, experts_here, capacity, block_width), jnp.bfloat16
        ),
        grid=(experts_here, steps),
        in_specs=[
            pl.BlockSpec((sections, None, capacity, hidden), lambda j, b: (0, j, 0, 0)),
            pl.BlockSpec((None, hidden, blocks_per_step * block_width), lambda j, b: (j, 0, b)),
        ],
        out_specs=pl.BlockSpec(
            (blocks_per_step, sections, None, capacity, block_width),
            lambda j, b: (b, 0, j, 0, 0),
        ),
        cost_estimate=pl.CostEstimate(
            flops=2 * sections * experts_here * capacity * hidden * features,
            bytes_accessed=2 * (hidden_act.size + down_weight.size + hidden_act.size // hidden * features),
            transcendentals=0,
        ),
    )(hidden_act, down_weight)


def exchange_kernel(x_ref, o_ref, send_sem, recv_sem, local_sem):
    n = x_ref.shape[0]
    me = lax.axis_index("seq")
    col = lax.axis_index("exp")
    mesh_id = pl.DeviceIdType.MESH
    barrier = pltpu.get_barrier_semaphore()
    for k in range(1, n):
        peer = lax.rem(me + k, n)
        pl.semaphore_signal(barrier, inc=1, device_id=(peer, col), device_id_type=mesh_id)
    pl.semaphore_wait(barrier, n - 1)
    local = pltpu.make_async_copy(x_ref.at[me], o_ref.at[me], local_sem)
    local.start()
    copies = []
    for k in range(1, n):
        peer = lax.rem(me + k, n)
        copy = pltpu.make_async_remote_copy(
            src_ref=x_ref.at[peer],
            dst_ref=o_ref.at[me],
            send_sem=send_sem.at[k],
            recv_sem=recv_sem.at[k],
            device_id=(peer, col),
            device_id_type=mesh_id,
        )
        copy.start()
        copies.append(copy)
    local.wait()
    for copy in copies:
        copy.wait()


def exchange(x, collective_id):
    n = x.shape[0]
    return pl.pallas_call(
        exchange_kernel,
        out_shape=jax.ShapeDtypeStruct(x.shape, x.dtype),
        in_specs=[pl.BlockSpec(memory_space=pltpu.VMEM)],
        out_specs=pl.BlockSpec(memory_space=pltpu.VMEM),
        scratch_shapes=[
            pltpu.SemaphoreType.DMA((n,)),
            pltpu.SemaphoreType.DMA((n,)),
            pltpu.SemaphoreType.DMA,
        ],
        compiler_params=pltpu.CompilerParams(collective_id=collective_id, has_side_effects=True),
    )(x)


def scan_kernel(x_ref, o_ref, state, received, send_sem, recv_sem):
    n = lax.axis_size("seq")
    me = lax.axis_index("seq")
    col = lax.axis_index("exp")
    mesh_id = pl.DeviceIdType.MESH
    size = x_ref.shape[1] - 8
    barrier = pltpu.get_barrier_semaphore()
    for k in range(1, n):
        peer = lax.rem(me + k, n)
        pl.semaphore_signal(barrier, inc=1, device_id=(peer, col), device_id_type=mesh_id)
    pl.semaphore_wait(barrier, n - 1)
    shifts = [1, 1, 2, 4]
    for r, d in enumerate(shifts):
        source = x_ref if r == 0 else state.at[r - 1]
        copies = []
        for h in range(x_ref.shape[0]):
            copy = pltpu.make_async_remote_copy(
                src_ref=source.at[h],
                dst_ref=received.at[r, h],
                send_sem=send_sem.at[r, h],
                recv_sem=recv_sem.at[r, h],
                device_id=(lax.rem(me + d, n), col),
                device_id_type=mesh_id,
            )
            copy.start()
            copies.append(copy)
        for copy in copies:
            copy.wait()
        has_input = me - d >= 0
        other = received[r]
        if r == 0:
            row = lax.broadcasted_iota(jnp.int32, other.shape, 1)
            identity = jnp.where(row < size, 0.0, 1.0).astype(jnp.float32)
            state[r] = jnp.where(has_input, other, identity)
        else:
            mine = state[r - 1]
            fade = mine[:, size : size + 1, :]
            combined_state = fade * other[:, :size, :] + mine[:, :size, :]
            combined_fade = mine[:, size:, :] * other[:, size:, :]
            state[r, :, :size, :] = jnp.where(has_input, combined_state, mine[:, :size, :])
            state[r, :, size:, :] = jnp.where(has_input, combined_fade, mine[:, size:, :])

    o_ref[...] = state[len(shifts) - 1, :, :size, :]


def incoming_state(packed):
    heads, rows, width = packed.shape
    steps = 4
    return pl.pallas_call(
        scan_kernel,
        out_shape=jax.ShapeDtypeStruct((heads, rows - 8, width), jnp.float32),
        in_specs=[pl.BlockSpec(memory_space=pltpu.VMEM)],
        out_specs=pl.BlockSpec(memory_space=pltpu.VMEM),
        scratch_shapes=[
            pltpu.VMEM((steps, heads, rows, width), jnp.float32),
            pltpu.VMEM((steps, heads, rows, width), jnp.float32),
            pltpu.SemaphoreType.DMA((steps, heads)),
            pltpu.SemaphoreType.DMA((steps, heads)),
        ],
        compiler_params=pltpu.CompilerParams(collective_id=2, has_side_effects=True),
    )(packed)


def on_device(
    attn_query,
    attn_key,
    attn_value,
    log_decay,
    residual,
    norm_gain,
    expert_ids,
    router_weight,
    gate_weight,
    up_weight,
    down_weight,
):
    heads_here = log_decay.shape[0]
    length = log_decay.shape[1]
    head_size = attn_query.shape[1] // heads_here
    query_rows = attn_query.reshape(length, heads_here, head_size)
    key_rows = attn_key.reshape(length, heads_here, head_size)
    value_rows = attn_value.reshape(length, heads_here, head_size)
    cumulative = jnp.cumsum(log_decay, axis=1)
    causal = lax.broadcasted_iota(jnp.int32, (length, length), 0) >= lax.broadcasted_iota(
        jnp.int32, (length, length), 1
    )
    decay_gap = jnp.where(causal[None], cumulative[:, :, None] - cumulative[:, None, :], 0.0)
    decay_mask = jnp.where(causal[None], jnp.exp(decay_gap), 0.0)
    scores = jnp.einsum("thd,shd->hts", query_rows, key_rows, preferred_element_type=jnp.float32)
    weights = (scores * decay_mask).astype(jnp.bfloat16)
    intra_part = jnp.einsum("hts,shd->thd", weights, value_rows, preferred_element_type=jnp.float32)
    key_fade = jnp.exp(cumulative[:, -1:] - cumulative)
    scaled = (key_fade.T[:, :, None] * key_rows.astype(jnp.float32)).astype(jnp.bfloat16)
    local_state = jnp.einsum("shd,she->hde", scaled, value_rows, preferred_element_type=jnp.float32)
    section_fade = jnp.exp(cumulative[:, -1])
    packed = jnp.concatenate(
        [local_state, jnp.broadcast_to(section_fade[:, None, None], (heads_here, 8, head_size))],
        axis=1,
    )
    incoming = incoming_state(packed)
    inter_part = jnp.einsum(
        "thd,hde->the", query_rows.astype(jnp.float32), incoming, precision=lax.Precision.HIGHEST
    )
    attn_out = intra_part + jnp.exp(cumulative).T[:, :, None] * inter_part
    mean_square = jnp.mean(attn_out * attn_out, axis=2, keepdims=True)
    normed = (attn_out / jnp.sqrt(mean_square + 1e-06)).reshape(length, heads_here * head_size)
    stream = (residual.astype(jnp.float32) + norm_gain.astype(jnp.float32) * normed).astype(
        jnp.bfloat16
    )
    experts_here = router_weight.shape[1]
    groups = lax.axis_size("seq")
    expert_count = experts_here * groups
    capacity = 4 * length // expert_count
    features = stream.shape[1]
    choices_per_token = expert_ids.shape[1]
    flat_ids = expert_ids.reshape(-1)
    expert_iota = lax.broadcasted_iota(jnp.int32, (1, expert_count), 1)
    onehot = (flat_ids[:, None] == expert_iota).astype(jnp.int32)
    running = jnp.cumsum(onehot, axis=0)
    slot_index = jnp.sum(running * onehot, axis=1) - 1
    target = flat_ids * capacity + slot_index
    place_iota = lax.broadcasted_iota(jnp.int32, (expert_count * capacity, 1), 0)
    route_matrix = (
        (place_iota == target[None, :])
        .astype(jnp.bfloat16)
        .reshape(expert_count * capacity, length, choices_per_token)
        .sum(axis=2)
    )
    outgoing = jnp.dot(route_matrix, stream, preferred_element_type=jnp.float32).astype(
        jnp.bfloat16
    )
    outgoing = outgoing.reshape(groups, experts_here, capacity, features)
    shards = lax.axis_size("exp")
    portion = lax.all_gather(
        exchange(outgoing, 0),
        "exp",
        axis=0,
    )
    hidden_units = gate_weight.shape[2]
    gate_blocks = gate_weight.reshape(experts_here, shards, features, hidden_units)
    up_blocks = up_weight.reshape(experts_here, shards, features, hidden_units)
    router_blocks = router_weight.reshape(shards, features, experts_here)
    gate_up = jnp.einsum(
        "esjcd,jedf->sjcf",
        portion,
        jnp.concatenate([gate_blocks, up_blocks], axis=3),
        preferred_element_type=jnp.float32,
    )
    gate_acc = gate_up[..., :hidden_units]
    upward = gate_up[..., hidden_units:]
    logits = jnp.einsum(
        "esjcd,edj->sjc", portion, router_blocks, preferred_element_type=jnp.float32
    )
    hidden_act = (jax.nn.silu(gate_acc) * upward).astype(jnp.bfloat16)
    expert_out = lax.psum_scatter(
        down_projection(hidden_act, down_weight, shards),
        "exp",
        scatter_dimension=0,
        tiled=True,
    )[0].astype(jnp.float32)
    routed = (jax.nn.sigmoid(logits)[..., None] * expert_out).astype(jnp.bfloat16)
    returned = exchange(routed, 1)
    returned = returned.reshape(expert_count * capacity, features)
    combined = lax.dot_general(
        route_matrix, returned, (((0,), (0,)), ((), ())), preferred_element_type=jnp.float32
    )
    return (stream.astype(jnp.float32) + combined).astype(jnp.bfloat16)


def solution(mesh):
    in_specs = (
        P("seq", "exp"),
        P("seq", "exp"),
        P("seq", "exp"),
        P("exp", "seq"),
        P("seq", "exp"),
        P("exp"),
        P("seq", None),
        P(None, "seq"),
        P("seq", None, "exp"),
        P("seq", None, "exp"),
        P("seq", "exp", None),
    )
    out_specs = P("seq", "exp")
    return jax.shard_map(
        on_device, mesh=mesh, in_specs=in_specs, out_specs=out_specs, check_vma=False
    )
```

```python
import functools

import jax
import jax.numpy as jnp
from jax import lax
from jax.sharding import PartitionSpec as P
from jax.experimental import pallas as pl
from jax.experimental.pallas import tpu as pltpu


def shifted(array, axis, by):
    count = lax.axis_size(axis)
    pairs = [(i, i + by) for i in range(count) if 0 <= i + by < count]
    return lax.ppermute(array, axis, pairs)


def down_kernel(blocks_per_step, block_width, h_ref, w_ref, o_ref):
    sections, capacity, hidden = h_ref.shape
    rows = h_ref[...].reshape(sections * capacity, hidden)
    product = jnp.dot(rows, w_ref[...], preferred_element_type=jnp.float32)
    for i in range(blocks_per_step):
        piece = product[:, i * block_width : (i + 1) * block_width]
        o_ref[i] = piece.astype(o_ref.dtype).reshape(sections, capacity, block_width)


def down_projection(hidden_act, down_weight, shards):
    sections, experts_here, capacity, hidden = hidden_act.shape
    features = down_weight.shape[2]
    block_width = features // shards
    blocks_per_step = 16
    steps = shards // blocks_per_step
    return pl.pallas_call(
        functools.partial(down_kernel, blocks_per_step, block_width),
        out_shape=jax.ShapeDtypeStruct(
            (shards, sections, experts_here, capacity, block_width), jnp.bfloat16
        ),
        grid=(experts_here, steps),
        in_specs=[
            pl.BlockSpec((sections, None, capacity, hidden), lambda j, b: (0, j, 0, 0)),
            pl.BlockSpec((None, hidden, blocks_per_step * block_width), lambda j, b: (j, 0, b)),
        ],
        out_specs=pl.BlockSpec(
            (blocks_per_step, sections, None, capacity, block_width),
            lambda j, b: (b, 0, j, 0, 0),
        ),
        cost_estimate=pl.CostEstimate(
            flops=2 * sections * experts_here * capacity * hidden * features,
            bytes_accessed=2 * (hidden_act.size + down_weight.size + hidden_act.size // hidden * features),
            transcendentals=0,
        ),
    )(hidden_act, down_weight)


def exchange_kernel(x_ref, o_ref, send_sem, recv_sem, local_sem):
    n = x_ref.shape[0]
    me = lax.axis_index("seq")
    col = lax.axis_index("exp")
    mesh_id = pl.DeviceIdType.MESH
    barrier = pltpu.get_barrier_semaphore()
    for k in range(1, n):
        peer = lax.rem(me + k, n)
        pl.semaphore_signal(barrier, inc=1, device_id=(peer, col), device_id_type=mesh_id)
    pl.semaphore_wait(barrier, n - 1)
    local = pltpu.make_async_copy(x_ref.at[me], o_ref.at[me], local_sem)
    local.start()
    copies = []
    for k in range(1, n):
        peer = lax.rem(me + k, n)
        copy = pltpu.make_async_remote_copy(
            src_ref=x_ref.at[peer],
            dst_ref=o_ref.at[me],
            send_sem=send_sem.at[k],
            recv_sem=recv_sem.at[k],
            device_id=(peer, col),
            device_id_type=mesh_id,
        )
        copy.start()
        copies.append(copy)
    local.wait()
    for copy in copies:
        copy.wait()


def exchange(x, collective_id):
    n = x.shape[0]
    return pl.pallas_call(
        exchange_kernel,
        out_shape=jax.ShapeDtypeStruct(x.shape, x.dtype),
        in_specs=[pl.BlockSpec(memory_space=pltpu.VMEM)],
        out_specs=pl.BlockSpec(memory_space=pltpu.VMEM),
        scratch_shapes=[
            pltpu.SemaphoreType.DMA((n,)),
            pltpu.SemaphoreType.DMA((n,)),
            pltpu.SemaphoreType.DMA,
        ],
        compiler_params=pltpu.CompilerParams(collective_id=collective_id, has_side_effects=True),
    )(x)


def scan_kernel(x_ref, o_ref, state, received, send_sem, recv_sem):
    n = lax.axis_size("seq")
    me = lax.axis_index("seq")
    col = lax.axis_index("exp")
    mesh_id = pl.DeviceIdType.MESH
    size = x_ref.shape[1] - 8
    barrier = pltpu.get_barrier_semaphore()
    for k in range(1, n):
        peer = lax.rem(me + k, n)
        pl.semaphore_signal(barrier, inc=1, device_id=(peer, col), device_id_type=mesh_id)
    pl.semaphore_wait(barrier, n - 1)
    shifts = [1, 1, 2, 4]
    for r, d in enumerate(shifts):
        source = x_ref if r == 0 else state.at[r - 1]
        copy = pltpu.make_async_remote_copy(
            src_ref=source,
            dst_ref=received.at[r],
            send_sem=send_sem.at[r],
            recv_sem=recv_sem.at[r],
            device_id=(lax.rem(me + d, n), col),
            device_id_type=mesh_id,
        )
        copy.start()
        copy.wait()
        has_input = me - d >= 0
        other = received[r]
        if r == 0:
            row = lax.broadcasted_iota(jnp.int32, other.shape, 1)
            identity = jnp.where(row < size, 0.0, 1.0).astype(jnp.float32)
            state[r] = jnp.where(has_input, other, identity)
        else:
            mine = state[r - 1]
            fade = mine[:, size : size + 1, :]
            combined_state = fade * other[:, :size, :] + mine[:, :size, :]
            combined_fade = mine[:, size:, :] * other[:, size:, :]
            state[r, :, :size, :] = jnp.where(has_input, combined_state, mine[:, :size, :])
            state[r, :, size:, :] = jnp.where(has_input, combined_fade, mine[:, size:, :])

    o_ref[...] = state[len(shifts) - 1, :, :size, :]


def incoming_state(packed):
    heads, rows, width = packed.shape
    steps = 4
    return pl.pallas_call(
        scan_kernel,
        out_shape=jax.ShapeDtypeStruct((heads, rows - 8, width), jnp.float32),
        in_specs=[pl.BlockSpec(memory_space=pltpu.VMEM)],
        out_specs=pl.BlockSpec(memory_space=pltpu.VMEM),
        scratch_shapes=[
            pltpu.VMEM((steps, heads, rows, width), jnp.float32),
            pltpu.VMEM((steps, heads, rows, width), jnp.float32),
            pltpu.SemaphoreType.DMA((steps,)),
            pltpu.SemaphoreType.DMA((steps,)),
        ],
        compiler_params=pltpu.CompilerParams(collective_id=2, has_side_effects=True),
    )(packed)


def on_device(
    attn_query,
    attn_key,
    attn_value,
    log_decay,
    residual,
    norm_gain,
    expert_ids,
    router_weight,
    gate_weight,
    up_weight,
    down_weight,
):
    heads_here = log_decay.shape[0]
    length = log_decay.shape[1]
    head_size = attn_query.shape[1] // heads_here
    query_rows = attn_query.reshape(length, heads_here, head_size)
    key_rows = attn_key.reshape(length, heads_here, head_size)
    value_rows = attn_value.reshape(length, heads_here, head_size)
    cumulative = jnp.cumsum(log_decay, axis=1)
    causal = lax.broadcasted_iota(jnp.int32, (length, length), 0) >= lax.broadcasted_iota(
        jnp.int32, (length, length), 1
    )
    decay_gap = jnp.where(causal[None], cumulative[:, :, None] - cumulative[:, None, :], 0.0)
    decay_mask = jnp.where(causal[None], jnp.exp(decay_gap), 0.0)
    scores = jnp.einsum("thd,shd->hts", query_rows, key_rows, preferred_element_type=jnp.float32)
    weights = (scores * decay_mask).astype(jnp.bfloat16)
    intra_part = jnp.einsum("hts,shd->thd", weights, value_rows, preferred_element_type=jnp.float32)
    key_fade = jnp.exp(cumulative[:, -1:] - cumulative)
    scaled = (key_fade.T[:, :, None] * key_rows.astype(jnp.float32)).astype(jnp.bfloat16)
    local_state = jnp.einsum("shd,she->hde", scaled, value_rows, preferred_element_type=jnp.float32)
    section_fade = jnp.exp(cumulative[:, -1])
    packed = jnp.concatenate(
        [local_state, jnp.broadcast_to(section_fade[:, None, None], (heads_here, 8, head_size))],
        axis=1,
    )
    incoming = incoming_state(packed)
    inter_part = jnp.einsum(
        "thd,hde->the", query_rows.astype(jnp.float32), incoming, precision=lax.Precision.HIGHEST
    )
    attn_out = intra_part + jnp.exp(cumulative).T[:, :, None] * inter_part
    mean_square = jnp.mean(attn_out * attn_out, axis=2, keepdims=True)
    normed = (attn_out / jnp.sqrt(mean_square + 1e-06)).reshape(length, heads_here * head_size)
    stream = (residual.astype(jnp.float32) + norm_gain.astype(jnp.float32) * normed).astype(
        jnp.bfloat16
    )
    experts_here = router_weight.shape[1]
    groups = lax.axis_size("seq")
    expert_count = experts_here * groups
    capacity = 4 * length // expert_count
    features = stream.shape[1]
    choices_per_token = expert_ids.shape[1]
    flat_ids = expert_ids.reshape(-1)
    expert_iota = lax.broadcasted_iota(jnp.int32, (1, expert_count), 1)
    onehot = (flat_ids[:, None] == expert_iota).astype(jnp.int32)
    running = jnp.cumsum(onehot, axis=0)
    slot_index = jnp.sum(running * onehot, axis=1) - 1
    target = flat_ids * capacity + slot_index
    place_iota = lax.broadcasted_iota(jnp.int32, (expert_count * capacity, 1), 0)
    route_matrix = (
        (place_iota == target[None, :])
        .astype(jnp.bfloat16)
        .reshape(expert_count * capacity, length, choices_per_token)
        .sum(axis=2)
    )
    outgoing = jnp.dot(route_matrix, stream, preferred_element_type=jnp.float32).astype(
        jnp.bfloat16
    )
    outgoing = outgoing.reshape(groups, experts_here, capacity, features)
    shards = lax.axis_size("exp")
    portion = lax.all_gather(
        exchange(outgoing, 0),
        "exp",
        axis=0,
    )
    hidden_units = gate_weight.shape[2]
    gate_blocks = gate_weight.reshape(experts_here, shards, features, hidden_units)
    up_blocks = up_weight.reshape(experts_here, shards, features, hidden_units)
    router_blocks = router_weight.reshape(shards, features, experts_here)
    gate_up = jnp.einsum(
        "esjcd,jedf->sjcf",
        portion,
        jnp.concatenate([gate_blocks, up_blocks], axis=3),
        preferred_element_type=jnp.float32,
    )
    gate_acc = gate_up[..., :hidden_units]
    upward = gate_up[..., hidden_units:]
    logits = jnp.einsum(
        "esjcd,edj->sjc", portion, router_blocks, preferred_element_type=jnp.float32
    )
    hidden_act = (jax.nn.silu(gate_acc) * upward).astype(jnp.bfloat16)
    expert_out = lax.psum_scatter(
        down_projection(hidden_act, down_weight, shards),
        "exp",
        scatter_dimension=0,
        tiled=True,
    )[0].astype(jnp.float32)
    routed = (jax.nn.sigmoid(logits)[..., None] * expert_out).astype(jnp.bfloat16)
    returned = exchange(routed, 1)
    returned = returned.reshape(expert_count * capacity, features)
    combined = lax.dot_general(
        route_matrix, returned, (((0,), (0,)), ((), ())), preferred_element_type=jnp.float32
    )
    return (stream.astype(jnp.float32) + combined).astype(jnp.bfloat16)


def solution(mesh):
    in_specs = (
        P("seq", "exp"),
        P("seq", "exp"),
        P("seq", "exp"),
        P("exp", "seq"),
        P("seq", "exp"),
        P("exp"),
        P("seq", None),
        P(None, "seq"),
        P("seq", None, "exp"),
        P("seq", None, "exp"),
        P("seq", "exp", None),
    )
    out_specs = P("seq", "exp")
    return jax.shard_map(
        on_device, mesh=mesh, in_specs=in_specs, out_specs=out_specs, check_vma=False
    )
```

```python
import functools

import jax
import jax.numpy as jnp
from jax import lax
from jax.sharding import PartitionSpec as P
from jax.experimental import pallas as pl
from jax.experimental.pallas import tpu as pltpu


def shifted(array, axis, by):
    count = lax.axis_size(axis)
    pairs = [(i, i + by) for i in range(count) if 0 <= i + by < count]
    return lax.ppermute(array, axis, pairs)


def down_kernel(blocks_per_step, block_width, h_ref, s_ref, w_ref, o_ref):
    sections, capacity, hidden = h_ref.shape
    rows = h_ref[...].reshape(sections * capacity, hidden)
    product = jnp.dot(rows, w_ref[...], preferred_element_type=jnp.float32)
    product = product * s_ref[...].reshape(sections * capacity, 1)
    for i in range(blocks_per_step):
        piece = product[:, i * block_width : (i + 1) * block_width]
        o_ref[i] = piece.astype(o_ref.dtype).reshape(sections, capacity, block_width)


def down_projection(hidden_act, scale, down_weight, shards):
    sections, experts_here, capacity, hidden = hidden_act.shape
    features = down_weight.shape[2]
    block_width = features // shards
    blocks_per_step = 8
    steps = shards // blocks_per_step
    return pl.pallas_call(
        functools.partial(down_kernel, blocks_per_step, block_width),
        out_shape=jax.ShapeDtypeStruct(
            (shards, sections, experts_here, capacity, block_width), jnp.bfloat16
        ),
        grid=(experts_here, steps),
        in_specs=[
            pl.BlockSpec((sections, None, capacity, hidden), lambda j, b: (0, j, 0, 0)),
            pl.BlockSpec((sections, None, capacity, 1), lambda j, b: (0, j, 0, 0)),
            pl.BlockSpec((None, hidden, blocks_per_step * block_width), lambda j, b: (j, 0, b)),
        ],
        out_specs=pl.BlockSpec(
            (blocks_per_step, sections, None, capacity, block_width),
            lambda j, b: (b, 0, j, 0, 0),
        ),
        cost_estimate=pl.CostEstimate(
            flops=2 * sections * experts_here * capacity * hidden * features,
            bytes_accessed=2 * (hidden_act.size + down_weight.size + hidden_act.size // hidden * features),
            transcendentals=0,
        ),
    )(hidden_act, scale, down_weight)


def exchange_kernel(x_ref, o_ref, send_sem, recv_sem, local_sem):
    n = x_ref.shape[0]
    me = lax.axis_index("seq")
    col = lax.axis_index("exp")
    mesh_id = pl.DeviceIdType.MESH
    barrier = pltpu.get_barrier_semaphore()
    for k in range(1, n):
        peer = lax.rem(me + k, n)
        pl.semaphore_signal(barrier, inc=1, device_id=(peer, col), device_id_type=mesh_id)
    pl.semaphore_wait(barrier, n - 1)
    local = pltpu.make_async_copy(x_ref.at[me], o_ref.at[me], local_sem)
    local.start()
    copies = []
    for k in range(1, n):
        peer = lax.rem(me + k, n)
        copy = pltpu.make_async_remote_copy(
            src_ref=x_ref.at[peer],
            dst_ref=o_ref.at[me],
            send_sem=send_sem.at[k],
            recv_sem=recv_sem.at[k],
            device_id=(peer, col),
            device_id_type=mesh_id,
        )
        copy.start()
        copies.append(copy)
    local.wait()
    for copy in copies:
        copy.wait()


def exchange(x, collective_id):
    n = x.shape[0]
    return pl.pallas_call(
        exchange_kernel,
        out_shape=jax.ShapeDtypeStruct(x.shape, x.dtype),
        in_specs=[pl.BlockSpec(memory_space=pltpu.VMEM)],
        out_specs=pl.BlockSpec(memory_space=pltpu.VMEM),
        scratch_shapes=[
            pltpu.SemaphoreType.DMA((n,)),
            pltpu.SemaphoreType.DMA((n,)),
            pltpu.SemaphoreType.DMA,
        ],
        compiler_params=pltpu.CompilerParams(collective_id=collective_id, has_side_effects=True),
    )(x)


def scan_kernel(x_ref, o_ref, state, received, send_sem, recv_sem):
    n = lax.axis_size("seq")
    me = lax.axis_index("seq")
    col = lax.axis_index("exp")
    mesh_id = pl.DeviceIdType.MESH
    size = x_ref.shape[1] - 8
    barrier = pltpu.get_barrier_semaphore()
    for k in range(1, n):
        peer = lax.rem(me + k, n)
        pl.semaphore_signal(barrier, inc=1, device_id=(peer, col), device_id_type=mesh_id)
    pl.semaphore_wait(barrier, n - 1)
    shifts = [1, 1, 2, 4]
    for r, d in enumerate(shifts):
        source = x_ref if r == 0 else state.at[r - 1]
        copy = pltpu.make_async_remote_copy(
            src_ref=source,
            dst_ref=received.at[r],
            send_sem=send_sem.at[r],
            recv_sem=recv_sem.at[r],
            device_id=(lax.rem(me + d, n), col),
            device_id_type=mesh_id,
        )
        copy.start()
        copy.wait()
        has_input = me - d >= 0
        other = received[r]
        if r == 0:
            row = lax.broadcasted_iota(jnp.int32, other.shape, 1)
            identity = jnp.where(row < size, 0.0, 1.0).astype(jnp.float32)
            state[r] = jnp.where(has_input, other, identity)
        else:
            mine = state[r - 1]
            fade = mine[:, size : size + 1, :]
            combined_state = fade * other[:, :size, :] + mine[:, :size, :]
            combined_fade = mine[:, size:, :] * other[:, size:, :]
            state[r, :, :size, :] = jnp.where(has_input, combined_state, mine[:, :size, :])
            state[r, :, size:, :] = jnp.where(has_input, combined_fade, mine[:, size:, :])

    o_ref[...] = state[len(shifts) - 1, :, :size, :]


def incoming_state(packed):
    heads, rows, width = packed.shape
    steps = 4
    return pl.pallas_call(
        scan_kernel,
        out_shape=jax.ShapeDtypeStruct((heads, rows - 8, width), jnp.float32),
        in_specs=[pl.BlockSpec(memory_space=pltpu.VMEM)],
        out_specs=pl.BlockSpec(memory_space=pltpu.VMEM),
        scratch_shapes=[
            pltpu.VMEM((steps, heads, rows, width), jnp.float32),
            pltpu.VMEM((steps, heads, rows, width), jnp.float32),
            pltpu.SemaphoreType.DMA((steps,)),
            pltpu.SemaphoreType.DMA((steps,)),
        ],
        compiler_params=pltpu.CompilerParams(collective_id=2, has_side_effects=True),
    )(packed)


def on_device(
    attn_query,
    attn_key,
    attn_value,
    log_decay,
    residual,
    norm_gain,
    expert_ids,
    router_weight,
    gate_weight,
    up_weight,
    down_weight,
):
    heads_here = log_decay.shape[0]
    length = log_decay.shape[1]
    head_size = attn_query.shape[1] // heads_here
    query_rows = attn_query.reshape(length, heads_here, head_size)
    key_rows = attn_key.reshape(length, heads_here, head_size)
    value_rows = attn_value.reshape(length, heads_here, head_size)
    cumulative = jnp.cumsum(log_decay, axis=1)
    causal = lax.broadcasted_iota(jnp.int32, (length, length), 0) >= lax.broadcasted_iota(
        jnp.int32, (length, length), 1
    )
    decay_gap = jnp.where(causal[None], cumulative[:, :, None] - cumulative[:, None, :], 0.0)
    decay_mask = jnp.where(causal[None], jnp.exp(decay_gap), 0.0)
    scores = jnp.einsum("thd,shd->hts", query_rows, key_rows, preferred_element_type=jnp.float32)
    weights = (scores * decay_mask).astype(jnp.bfloat16)
    intra_part = jnp.einsum("hts,shd->thd", weights, value_rows, preferred_element_type=jnp.float32)
    key_fade = jnp.exp(cumulative[:, -1:] - cumulative)
    scaled = (key_fade.T[:, :, None] * key_rows.astype(jnp.float32)).astype(jnp.bfloat16)
    local_state = jnp.einsum("shd,she->hde", scaled, value_rows, preferred_element_type=jnp.float32)
    section_fade = jnp.exp(cumulative[:, -1])
    packed = jnp.concatenate(
        [local_state, jnp.broadcast_to(section_fade[:, None, None], (heads_here, 8, head_size))],
        axis=1,
    )
    incoming = incoming_state(packed)
    inter_part = jnp.einsum(
        "thd,hde->the", query_rows.astype(jnp.float32), incoming, precision=lax.Precision.HIGHEST
    )
    attn_out = intra_part + jnp.exp(cumulative).T[:, :, None] * inter_part
    mean_square = jnp.mean(attn_out * attn_out, axis=2, keepdims=True)
    normed = (attn_out / jnp.sqrt(mean_square + 1e-06)).reshape(length, heads_here * head_size)
    stream = (residual.astype(jnp.float32) + norm_gain.astype(jnp.float32) * normed).astype(
        jnp.bfloat16
    )
    experts_here = router_weight.shape[1]
    groups = lax.axis_size("seq")
    expert_count = experts_here * groups
    capacity = 4 * length // expert_count
    features = stream.shape[1]
    choices_per_token = expert_ids.shape[1]
    flat_ids = expert_ids.reshape(-1)
    expert_iota = lax.broadcasted_iota(jnp.int32, (1, expert_count), 1)
    onehot = (flat_ids[:, None] == expert_iota).astype(jnp.int32)
    running = jnp.cumsum(onehot, axis=0)
    slot_index = jnp.sum(running * onehot, axis=1) - 1
    target = flat_ids * capacity + slot_index
    place_iota = lax.broadcasted_iota(jnp.int32, (expert_count * capacity, 1), 0)
    route_matrix = (
        (place_iota == target[None, :])
        .astype(jnp.bfloat16)
        .reshape(expert_count * capacity, length, choices_per_token)
        .sum(axis=2)
    )
    outgoing = jnp.dot(route_matrix, stream, preferred_element_type=jnp.float32).astype(
        jnp.bfloat16
    )
    outgoing = outgoing.reshape(groups, experts_here, capacity, features)
    shards = lax.axis_size("exp")
    portion = lax.all_gather(
        exchange(outgoing, 0),
        "exp",
        axis=0,
    )
    hidden_units = gate_weight.shape[2]
    gate_blocks = gate_weight.reshape(experts_here, shards, features, hidden_units)
    up_blocks = up_weight.reshape(experts_here, shards, features, hidden_units)
    router_blocks = router_weight.reshape(shards, features, experts_here)
    router_columns = router_blocks.transpose(2, 0, 1)[..., None]
    gate_up = jnp.einsum(
        "esjcd,jedf->sjcf",
        portion,
        jnp.concatenate([gate_blocks, up_blocks, router_columns], axis=3),
        preferred_element_type=jnp.float32,
    )
    gate_acc = gate_up[..., :hidden_units]
    upward = gate_up[..., hidden_units : 2 * hidden_units]
    logits = gate_up[..., 2 * hidden_units]
    hidden_act = (jax.nn.silu(gate_acc) * upward).astype(jnp.bfloat16)
    expert_out = lax.psum_scatter(
        down_projection(hidden_act, jax.nn.sigmoid(logits)[..., None], down_weight, shards),
        "exp",
        scatter_dimension=0,
        tiled=True,
    )[0]
    routed = expert_out
    returned = exchange(routed, 1)
    returned = returned.reshape(expert_count * capacity, features)
    combined = lax.dot_general(
        route_matrix, returned, (((0,), (0,)), ((), ())), preferred_element_type=jnp.float32
    )
    return (stream.astype(jnp.float32) + combined).astype(jnp.bfloat16)


def solution(mesh):
    in_specs = (
        P("seq", "exp"),
        P("seq", "exp"),
        P("seq", "exp"),
        P("exp", "seq"),
        P("seq", "exp"),
        P("exp"),
        P("seq", None),
        P(None, "seq"),
        P("seq", None, "exp"),
        P("seq", None, "exp"),
        P("seq", "exp", None),
    )
    out_specs = P("seq", "exp")
    return jax.shard_map(
        on_device, mesh=mesh, in_specs=in_specs, out_specs=out_specs, check_vma=False
    )
```

```python
import functools

import jax
import jax.numpy as jnp
from jax import lax
from jax.sharding import PartitionSpec as P
from jax.experimental import pallas as pl
from jax.experimental.pallas import tpu as pltpu


def shifted(array, axis, by):
    count = lax.axis_size(axis)
    pairs = [(i, i + by) for i in range(count) if 0 <= i + by < count]
    return lax.ppermute(array, axis, pairs)


def down_kernel(blocks_per_step, block_width, h_ref, w_ref, o_ref):
    sections, capacity, hidden = h_ref.shape
    rows = h_ref[...].reshape(sections * capacity, hidden)
    product = jnp.dot(rows, w_ref[...], preferred_element_type=jnp.float32)
    for i in range(blocks_per_step):
        piece = product[:, i * block_width : (i + 1) * block_width]
        o_ref[i] = piece.astype(o_ref.dtype).reshape(sections, capacity, block_width)


def down_projection(hidden_act, down_weight, shards):
    sections, experts_here, capacity, hidden = hidden_act.shape
    features = down_weight.shape[2]
    block_width = features // shards
    blocks_per_step = 8
    steps = shards // blocks_per_step
    return pl.pallas_call(
        functools.partial(down_kernel, blocks_per_step, block_width),
        out_shape=jax.ShapeDtypeStruct(
            (shards, sections, experts_here, capacity, block_width), jnp.bfloat16
        ),
        grid=(experts_here, steps),
        in_specs=[
            pl.BlockSpec((sections, None, capacity, hidden), lambda j, b: (0, j, 0, 0)),
            pl.BlockSpec((None, hidden, blocks_per_step * block_width), lambda j, b: (j, 0, b)),
        ],
        out_specs=pl.BlockSpec(
            (blocks_per_step, sections, None, capacity, block_width),
            lambda j, b: (b, 0, j, 0, 0),
        ),
        cost_estimate=pl.CostEstimate(
            flops=2 * sections * experts_here * capacity * hidden * features,
            bytes_accessed=2 * (hidden_act.size + down_weight.size + hidden_act.size // hidden * features),
            transcendentals=0,
        ),
    )(hidden_act, down_weight)


def exchange_kernel(spread, x_ref, o_ref, send_sem, recv_sem, local_sem):
    n = o_ref.shape[0]
    me = lax.axis_index("seq")
    col = lax.axis_index("exp")
    mesh_id = pl.DeviceIdType.MESH
    barrier = pltpu.get_barrier_semaphore()
    for k in range(1, n):
        peer = lax.rem(me + k, n)
        pl.semaphore_signal(barrier, inc=1, device_id=(peer, col), device_id_type=mesh_id)
    pl.semaphore_wait(barrier, n - 1)
    local = pltpu.make_async_copy(x_ref if spread else x_ref.at[me], o_ref.at[me], local_sem)
    local.start()
    copies = []
    for k in range(1, n):
        peer = lax.rem(me + k, n)
        copy = pltpu.make_async_remote_copy(
            src_ref=x_ref if spread else x_ref.at[peer],
            dst_ref=o_ref.at[me],
            send_sem=send_sem.at[k],
            recv_sem=recv_sem.at[k],
            device_id=(peer, col),
            device_id_type=mesh_id,
        )
        copy.start()
        copies.append(copy)
    local.wait()
    for copy in copies:
        copy.wait()


def exchange(x, collective_id, spread=False):
    n = lax.axis_size("seq") if spread else x.shape[0]
    shape = (n,) + x.shape if spread else x.shape
    return pl.pallas_call(
        functools.partial(exchange_kernel, spread),
        out_shape=jax.ShapeDtypeStruct(shape, x.dtype),
        in_specs=[pl.BlockSpec(memory_space=pltpu.VMEM)],
        out_specs=pl.BlockSpec(memory_space=pltpu.VMEM),
        scratch_shapes=[
            pltpu.SemaphoreType.DMA((n,)),
            pltpu.SemaphoreType.DMA((n,)),
            pltpu.SemaphoreType.DMA,
        ],
        compiler_params=pltpu.CompilerParams(collective_id=collective_id, has_side_effects=True),
    )(x)


def on_device(
    attn_query,
    attn_key,
    attn_value,
    log_decay,
    residual,
    norm_gain,
    expert_ids,
    router_weight,
    gate_weight,
    up_weight,
    down_weight,
):
    heads_here = log_decay.shape[0]
    length = log_decay.shape[1]
    head_size = attn_query.shape[1] // heads_here
    query_rows = attn_query.reshape(length, heads_here, head_size)
    key_rows = attn_key.reshape(length, heads_here, head_size)
    value_rows = attn_value.reshape(length, heads_here, head_size)
    cumulative = jnp.cumsum(log_decay, axis=1)
    causal = lax.broadcasted_iota(jnp.int32, (length, length), 0) >= lax.broadcasted_iota(
        jnp.int32, (length, length), 1
    )
    decay_gap = jnp.where(causal[None], cumulative[:, :, None] - cumulative[:, None, :], 0.0)
    decay_mask = jnp.where(causal[None], jnp.exp(decay_gap), 0.0)
    scores = jnp.einsum("thd,shd->hts", query_rows, key_rows, preferred_element_type=jnp.float32)
    weights = (scores * decay_mask).astype(jnp.bfloat16)
    intra_part = jnp.einsum("hts,shd->thd", weights, value_rows, preferred_element_type=jnp.float32)
    key_fade = jnp.exp(cumulative[:, -1:] - cumulative)
    scaled = (key_fade.T[:, :, None] * key_rows.astype(jnp.float32)).astype(jnp.bfloat16)
    local_state = jnp.einsum("shd,she->hde", scaled, value_rows, preferred_element_type=jnp.float32)
    section_log_fade = cumulative[:, -1]
    sections_total = lax.axis_size("seq")
    packed = jnp.concatenate(
        [local_state, jnp.broadcast_to(section_log_fade[:, None, None], (heads_here, 8, head_size))],
        axis=1,
    )
    gathered = exchange(packed, 2, spread=True)
    all_states = gathered[:, :, :head_size, :]
    all_log_fades = gathered[:, :, head_size, 0]
    me = lax.axis_index("seq")
    section_iota = lax.broadcasted_iota(jnp.int32, (sections_total, sections_total), 0)
    between_iota = lax.broadcasted_iota(jnp.int32, (sections_total, sections_total), 1)
    between = (between_iota > section_iota) & (between_iota < me)
    log_weight = jnp.sum(
        jnp.where(between[:, :, None], all_log_fades[None, :, :], 0.0), axis=1
    )
    state_weight = jnp.where(
        lax.broadcasted_iota(jnp.int32, (sections_total, 1), 0) < me, jnp.exp(log_weight), 0.0
    )
    incoming = jnp.sum(state_weight[:, :, None, None] * all_states, axis=0)
    inter_part = jnp.einsum(
        "thd,hde->the", query_rows.astype(jnp.float32), incoming, precision=lax.Precision.HIGHEST
    )
    attn_out = intra_part + jnp.exp(cumulative).T[:, :, None] * inter_part
    mean_square = jnp.mean(attn_out * attn_out, axis=2, keepdims=True)
    normed = (attn_out / jnp.sqrt(mean_square + 1e-06)).reshape(length, heads_here * head_size)
    stream = (residual.astype(jnp.float32) + norm_gain.astype(jnp.float32) * normed).astype(
        jnp.bfloat16
    )
    experts_here = router_weight.shape[1]
    groups = lax.axis_size("seq")
    expert_count = experts_here * groups
    capacity = 4 * length // expert_count
    features = stream.shape[1]
    choices_per_token = expert_ids.shape[1]
    flat_ids = expert_ids.reshape(-1)
    expert_iota = lax.broadcasted_iota(jnp.int32, (1, expert_count), 1)
    onehot = (flat_ids[:, None] == expert_iota).astype(jnp.int32)
    running = jnp.cumsum(onehot, axis=0)
    slot_index = jnp.sum(running * onehot, axis=1) - 1
    target = flat_ids * capacity + slot_index
    place_iota = lax.broadcasted_iota(jnp.int32, (expert_count * capacity, 1), 0)
    route_matrix = (
        (place_iota == target[None, :])
        .astype(jnp.bfloat16)
        .reshape(expert_count * capacity, length, choices_per_token)
        .sum(axis=2)
    )
    outgoing = jnp.dot(route_matrix, stream, preferred_element_type=jnp.float32).astype(
        jnp.bfloat16
    )
    outgoing = outgoing.reshape(groups, experts_here, capacity, features)
    shards = lax.axis_size("exp")
    portion = lax.all_gather(
        exchange(outgoing, 0),
        "exp",
        axis=0,
    )
    hidden_units = gate_weight.shape[2]
    gate_blocks = gate_weight.reshape(experts_here, shards, features, hidden_units)
    up_blocks = up_weight.reshape(experts_here, shards, features, hidden_units)
    router_blocks = router_weight.reshape(shards, features, experts_here)
    gate_up = jnp.einsum(
        "esjcd,jedf->sjcf",
        portion,
        jnp.concatenate([gate_blocks, up_blocks], axis=3),
        preferred_element_type=jnp.float32,
    )
    gate_acc = gate_up[..., :hidden_units]
    upward = gate_up[..., hidden_units:]
    logits = jnp.einsum(
        "esjcd,edj->sjc", portion, router_blocks, preferred_element_type=jnp.float32
    )
    hidden_act = (jax.nn.silu(gate_acc) * upward).astype(jnp.bfloat16)
    expert_out = lax.psum_scatter(
        down_projection(hidden_act, down_weight, shards),
        "exp",
        scatter_dimension=0,
        tiled=True,
    )[0].astype(jnp.float32)
    routed = (jax.nn.sigmoid(logits)[..., None] * expert_out).astype(jnp.bfloat16)
    returned = exchange(routed, 1)
    returned = returned.reshape(expert_count * capacity, features)
    combined = lax.dot_general(
        route_matrix, returned, (((0,), (0,)), ((), ())), preferred_element_type=jnp.float32
    )
    return (stream.astype(jnp.float32) + combined).astype(jnp.bfloat16)


def solution(mesh):
    in_specs = (
        P("seq", "exp"),
        P("seq", "exp"),
        P("seq", "exp"),
        P("exp", "seq"),
        P("seq", "exp"),
        P("exp"),
        P("seq", None),
        P(None, "seq"),
        P("seq", None, "exp"),
        P("seq", None, "exp"),
        P("seq", "exp", None),
    )
    out_specs = P("seq", "exp")
    return jax.shard_map(
        on_device, mesh=mesh, in_specs=in_specs, out_specs=out_specs, check_vma=False
    )
```

```python
import functools

import jax
import jax.numpy as jnp
from jax import lax
from jax.sharding import PartitionSpec as P
from jax.experimental import pallas as pl
from jax.experimental.pallas import tpu as pltpu


def shifted(array, axis, by):
    count = lax.axis_size(axis)
    pairs = [(i, i + by) for i in range(count) if 0 <= i + by < count]
    return lax.ppermute(array, axis, pairs)


def down_kernel(blocks_per_step, block_width, h_ref, w_ref, o_ref):
    sections, capacity, hidden = h_ref.shape
    rows = h_ref[...].reshape(sections * capacity, hidden)
    product = jnp.dot(rows, w_ref[...], preferred_element_type=jnp.float32)
    for i in range(blocks_per_step):
        piece = product[:, i * block_width : (i + 1) * block_width]
        o_ref[i] = piece.astype(o_ref.dtype).reshape(sections, capacity, block_width)


def down_projection(hidden_act, down_weight, shards):
    sections, experts_here, capacity, hidden = hidden_act.shape
    features = down_weight.shape[2]
    block_width = features // shards
    blocks_per_step = 8
    steps = shards // blocks_per_step
    return pl.pallas_call(
        functools.partial(down_kernel, blocks_per_step, block_width),
        out_shape=jax.ShapeDtypeStruct(
            (shards, sections, experts_here, capacity, block_width), jnp.bfloat16
        ),
        grid=(experts_here, steps),
        in_specs=[
            pl.BlockSpec((sections, None, capacity, hidden), lambda j, b: (0, j, 0, 0)),
            pl.BlockSpec((None, hidden, blocks_per_step * block_width), lambda j, b: (j, 0, b)),
        ],
        out_specs=pl.BlockSpec(
            (blocks_per_step, sections, None, capacity, block_width),
            lambda j, b: (b, 0, j, 0, 0),
        ),
        cost_estimate=pl.CostEstimate(
            flops=2 * sections * experts_here * capacity * hidden * features,
            bytes_accessed=2 * (hidden_act.size + down_weight.size + hidden_act.size // hidden * features),
            transcendentals=0,
        ),
    )(hidden_act, down_weight)


def exchange_kernel(x_ref, o_ref, send_sem, recv_sem, local_sem):
    n = x_ref.shape[0]
    me = lax.axis_index("seq")
    col = lax.axis_index("exp")
    mesh_id = pl.DeviceIdType.MESH
    barrier = pltpu.get_barrier_semaphore()
    for k in range(1, n):
        peer = lax.rem(me + k, n)
        pl.semaphore_signal(barrier, inc=1, device_id=(peer, col), device_id_type=mesh_id)
    pl.semaphore_wait(barrier, n - 1)
    local = pltpu.make_async_copy(x_ref.at[me], o_ref.at[me], local_sem)
    local.start()
    copies = []
    for k in range(1, n):
        peer = lax.rem(me + k, n)
        copy = pltpu.make_async_remote_copy(
            src_ref=x_ref.at[peer],
            dst_ref=o_ref.at[me],
            send_sem=send_sem.at[k],
            recv_sem=recv_sem.at[k],
            device_id=(peer, col),
            device_id_type=mesh_id,
        )
        copy.start()
        copies.append(copy)
    local.wait()
    for copy in copies:
        copy.wait()


def exchange(x, collective_id):
    n = x.shape[0]
    return pl.pallas_call(
        exchange_kernel,
        out_shape=jax.ShapeDtypeStruct(x.shape, x.dtype),
        in_specs=[pl.BlockSpec(memory_space=pltpu.VMEM)],
        out_specs=pl.BlockSpec(memory_space=pltpu.VMEM),
        scratch_shapes=[
            pltpu.SemaphoreType.DMA((n,)),
            pltpu.SemaphoreType.DMA((n,)),
            pltpu.SemaphoreType.DMA,
        ],
        compiler_params=pltpu.CompilerParams(collective_id=collective_id, has_side_effects=True),
    )(x)


def scan_kernel(x_ref, o_ref, state, received, send_sem, recv_sem):
    n = lax.axis_size("seq")
    me = lax.axis_index("seq")
    col = lax.axis_index("exp")
    mesh_id = pl.DeviceIdType.MESH
    size = x_ref.shape[1] - 8
    barrier = pltpu.get_barrier_semaphore()
    for k in range(1, n):
        peer = lax.rem(me + k, n)
        pl.semaphore_signal(barrier, inc=1, device_id=(peer, col), device_id_type=mesh_id)
    pl.semaphore_wait(barrier, n - 1)
    shifts = [1, 1, 2, 4]
    sent = []
    for r, d in enumerate(shifts):
        source = x_ref if r == 0 else state.at[r - 1]
        copy = pltpu.make_async_remote_copy(
            src_ref=source,
            dst_ref=received.at[r],
            send_sem=send_sem.at[r],
            recv_sem=recv_sem.at[r],
            device_id=(lax.rem(me + d, n), col),
            device_id_type=mesh_id,
        )
        copy.start()
        sent.append(copy)
        copy.wait_recv()
        has_input = me - d >= 0
        other = received[r]
        if r == 0:
            row = lax.broadcasted_iota(jnp.int32, other.shape, 1)
            identity = jnp.where(row < size, 0.0, 1.0).astype(jnp.float32)
            state[r] = jnp.where(has_input, other, identity)
        else:
            mine = state[r - 1]
            fade = mine[:, size : size + 1, :]
            combined_state = fade * other[:, :size, :] + mine[:, :size, :]
            combined_fade = mine[:, size:, :] * other[:, size:, :]
            state[r, :, :size, :] = jnp.where(has_input, combined_state, mine[:, :size, :])
            state[r, :, size:, :] = jnp.where(has_input, combined_fade, mine[:, size:, :])

    o_ref[...] = state[len(shifts) - 1, :, :size, :]
    for copy in sent:
        copy.wait_send()


def incoming_state(packed):
    heads, rows, width = packed.shape
    steps = 4
    return pl.pallas_call(
        scan_kernel,
        out_shape=jax.ShapeDtypeStruct((heads, rows - 8, width), jnp.float32),
        in_specs=[pl.BlockSpec(memory_space=pltpu.VMEM)],
        out_specs=pl.BlockSpec(memory_space=pltpu.VMEM),
        scratch_shapes=[
            pltpu.VMEM((steps, heads, rows, width), jnp.float32),
            pltpu.VMEM((steps, heads, rows, width), jnp.float32),
            pltpu.SemaphoreType.DMA((steps,)),
            pltpu.SemaphoreType.DMA((steps,)),
        ],
        compiler_params=pltpu.CompilerParams(collective_id=2, has_side_effects=True),
    )(packed)


def on_device(
    attn_query,
    attn_key,
    attn_value,
    log_decay,
    residual,
    norm_gain,
    expert_ids,
    router_weight,
    gate_weight,
    up_weight,
    down_weight,
):
    heads_here = log_decay.shape[0]
    length = log_decay.shape[1]
    head_size = attn_query.shape[1] // heads_here
    query_rows = attn_query.reshape(length, heads_here, head_size)
    key_rows = attn_key.reshape(length, heads_here, head_size)
    value_rows = attn_value.reshape(length, heads_here, head_size)
    cumulative = jnp.cumsum(log_decay, axis=1)
    causal = lax.broadcasted_iota(jnp.int32, (length, length), 0) >= lax.broadcasted_iota(
        jnp.int32, (length, length), 1
    )
    decay_gap = jnp.where(causal[None], cumulative[:, :, None] - cumulative[:, None, :], 0.0)
    decay_mask = jnp.where(causal[None], jnp.exp(decay_gap), 0.0)
    scores = jnp.einsum("thd,shd->hts", query_rows, key_rows, preferred_element_type=jnp.float32)
    weights = (scores * decay_mask).astype(jnp.bfloat16)
    intra_part = jnp.einsum("hts,shd->thd", weights, value_rows, preferred_element_type=jnp.float32)
    key_fade = jnp.exp(cumulative[:, -1:] - cumulative)
    scaled = (key_fade.T[:, :, None] * key_rows.astype(jnp.float32)).astype(jnp.bfloat16)
    local_state = jnp.einsum("shd,she->hde", scaled, value_rows, preferred_element_type=jnp.float32)
    section_fade = jnp.exp(cumulative[:, -1])
    packed = jnp.concatenate(
        [local_state, jnp.broadcast_to(section_fade[:, None, None], (heads_here, 8, head_size))],
        axis=1,
    )
    incoming = incoming_state(packed)
    inter_part = jnp.einsum(
        "thd,hde->the", query_rows.astype(jnp.float32), incoming, precision=lax.Precision.HIGHEST
    )
    attn_out = intra_part + jnp.exp(cumulative).T[:, :, None] * inter_part
    mean_square = jnp.mean(attn_out * attn_out, axis=2, keepdims=True)
    normed = (attn_out / jnp.sqrt(mean_square + 1e-06)).reshape(length, heads_here * head_size)
    stream = (residual.astype(jnp.float32) + norm_gain.astype(jnp.float32) * normed).astype(
        jnp.bfloat16
    )
    experts_here = router_weight.shape[1]
    groups = lax.axis_size("seq")
    expert_count = experts_here * groups
    capacity = 4 * length // expert_count
    features = stream.shape[1]
    choices_per_token = expert_ids.shape[1]
    flat_ids = expert_ids.reshape(-1)
    expert_iota = lax.broadcasted_iota(jnp.int32, (1, expert_count), 1)
    onehot = (flat_ids[:, None] == expert_iota).astype(jnp.int32)
    running = jnp.cumsum(onehot, axis=0)
    slot_index = jnp.sum(running * onehot, axis=1) - 1
    target = flat_ids * capacity + slot_index
    place_iota = lax.broadcasted_iota(jnp.int32, (expert_count * capacity, 1), 0)
    route_matrix = (
        (place_iota == target[None, :])
        .astype(jnp.bfloat16)
        .reshape(expert_count * capacity, length, choices_per_token)
        .sum(axis=2)
    )
    outgoing = jnp.dot(route_matrix, stream, preferred_element_type=jnp.float32).astype(
        jnp.bfloat16
    )
    outgoing = outgoing.reshape(groups, experts_here, capacity, features)
    shards = lax.axis_size("exp")
    portion = lax.all_gather(
        exchange(outgoing, 0),
        "exp",
        axis=0,
    )
    hidden_units = gate_weight.shape[2]
    gate_blocks = gate_weight.reshape(experts_here, shards, features, hidden_units)
    up_blocks = up_weight.reshape(experts_here, shards, features, hidden_units)
    router_blocks = router_weight.reshape(shards, features, experts_here)
    gate_up = jnp.einsum(
        "esjcd,jedf->sjcf",
        portion,
        jnp.concatenate([gate_blocks, up_blocks], axis=3),
        preferred_element_type=jnp.float32,
    )
    gate_acc = gate_up[..., :hidden_units]
    upward = gate_up[..., hidden_units:]
    logits = jnp.einsum(
        "esjcd,edj->sjc", portion, router_blocks, preferred_element_type=jnp.float32
    )
    hidden_act = (jax.nn.silu(gate_acc) * upward).astype(jnp.bfloat16)
    expert_out = lax.psum_scatter(
        down_projection(hidden_act, down_weight, shards),
        "exp",
        scatter_dimension=0,
        tiled=True,
    )[0].astype(jnp.float32)
    routed = (jax.nn.sigmoid(logits)[..., None] * expert_out).astype(jnp.bfloat16)
    returned = exchange(routed, 1)
    returned = returned.reshape(expert_count * capacity, features)
    combined = lax.dot_general(
        route_matrix, returned, (((0,), (0,)), ((), ())), preferred_element_type=jnp.float32
    )
    return (stream.astype(jnp.float32) + combined).astype(jnp.bfloat16)


def solution(mesh):
    in_specs = (
        P("seq", "exp"),
        P("seq", "exp"),
        P("seq", "exp"),
        P("exp", "seq"),
        P("seq", "exp"),
        P("exp"),
        P("seq", None),
        P(None, "seq"),
        P("seq", None, "exp"),
        P("seq", None, "exp"),
        P("seq", "exp", None),
    )
    out_specs = P("seq", "exp")
    return jax.shard_map(
        on_device, mesh=mesh, in_specs=in_specs, out_specs=out_specs, check_vma=False
    )
```

```python
import functools

import jax
import jax.numpy as jnp
from jax import lax
from jax.sharding import PartitionSpec as P
from jax.experimental import pallas as pl
from jax.experimental.pallas import tpu as pltpu


def shifted(array, axis, by):
    count = lax.axis_size(axis)
    pairs = [(i, i + by) for i in range(count) if 0 <= i + by < count]
    return lax.ppermute(array, axis, pairs)


def down_kernel(blocks_per_step, block_width, h_ref, w_ref, o_ref):
    sections, capacity, hidden = h_ref.shape
    rows = h_ref[...].reshape(sections * capacity, hidden)
    product = jnp.dot(rows, w_ref[...], preferred_element_type=jnp.float32)
    for i in range(blocks_per_step):
        piece = product[:, i * block_width : (i + 1) * block_width]
        o_ref[i] = piece.astype(o_ref.dtype).reshape(sections, capacity, block_width)


def down_projection(hidden_act, down_weight, shards):
    sections, experts_here, capacity, hidden = hidden_act.shape
    features = down_weight.shape[2]
    block_width = features // shards
    blocks_per_step = 8
    steps = shards // blocks_per_step
    return pl.pallas_call(
        functools.partial(down_kernel, blocks_per_step, block_width),
        out_shape=jax.ShapeDtypeStruct(
            (shards, sections, experts_here, capacity, block_width), jnp.bfloat16
        ),
        grid=(experts_here, steps),
        in_specs=[
            pl.BlockSpec((sections, None, capacity, hidden), lambda j, b: (0, j, 0, 0)),
            pl.BlockSpec((None, hidden, blocks_per_step * block_width), lambda j, b: (j, 0, b)),
        ],
        out_specs=pl.BlockSpec(
            (blocks_per_step, sections, None, capacity, block_width),
            lambda j, b: (b, 0, j, 0, 0),
        ),
        cost_estimate=pl.CostEstimate(
            flops=2 * sections * experts_here * capacity * hidden * features,
            bytes_accessed=2 * (hidden_act.size + down_weight.size + hidden_act.size // hidden * features),
            transcendentals=0,
        ),
    )(hidden_act, down_weight)


def exchange_kernel(x_ref, o_ref, send_sem, recv_sem, local_sem):
    n = x_ref.shape[0]
    me = lax.axis_index("seq")
    col = lax.axis_index("exp")
    mesh_id = pl.DeviceIdType.MESH
    barrier = pltpu.get_barrier_semaphore()
    for k in range(1, n):
        peer = lax.rem(me + k, n)
        pl.semaphore_signal(barrier, inc=1, device_id=(peer, col), device_id_type=mesh_id)
    pl.semaphore_wait(barrier, n - 1)
    local = pltpu.make_async_copy(x_ref.at[me], o_ref.at[me], local_sem)
    local.start()
    copies = []
    for k in range(1, n):
        peer = lax.rem(me + k, n)
        copy = pltpu.make_async_remote_copy(
            src_ref=x_ref.at[peer],
            dst_ref=o_ref.at[me],
            send_sem=send_sem.at[k],
            recv_sem=recv_sem.at[k],
            device_id=(peer, col),
            device_id_type=mesh_id,
        )
        copy.start()
        copies.append(copy)
    local.wait()
    for copy in copies:
        copy.wait()


def exchange(x, collective_id):
    n = x.shape[0]
    return pl.pallas_call(
        exchange_kernel,
        out_shape=jax.ShapeDtypeStruct(x.shape, x.dtype),
        in_specs=[pl.BlockSpec(memory_space=pltpu.VMEM)],
        out_specs=pl.BlockSpec(memory_space=pltpu.VMEM),
        scratch_shapes=[
            pltpu.SemaphoreType.DMA((n,)),
            pltpu.SemaphoreType.DMA((n,)),
            pltpu.SemaphoreType.DMA,
        ],
        compiler_params=pltpu.CompilerParams(collective_id=collective_id, has_side_effects=True),
    )(x)


def scan_kernel(x_ref, o_ref, state, received, send_sem, recv_sem):
    n = lax.axis_size("seq")
    me = lax.axis_index("seq")
    col = lax.axis_index("exp")
    mesh_id = pl.DeviceIdType.MESH
    size = x_ref.shape[1] - 8
    barrier = pltpu.get_barrier_semaphore()
    partners = [1, n - 1, 2, n - 2, 4]
    for k in partners:
        peer = lax.rem(me + k, n)
        pl.semaphore_signal(barrier, inc=1, device_id=(peer, col), device_id_type=mesh_id)
    pl.semaphore_wait(barrier, len(partners))
    shifts = [1, 1, 2, 4]
    for r, d in enumerate(shifts):
        source = x_ref if r == 0 else state.at[r - 1]
        copy = pltpu.make_async_remote_copy(
            src_ref=source,
            dst_ref=received.at[r],
            send_sem=send_sem.at[r],
            recv_sem=recv_sem.at[r],
            device_id=(lax.rem(me + d, n), col),
            device_id_type=mesh_id,
        )
        copy.start()
        copy.wait()
        has_input = me - d >= 0
        other = received[r]
        if r == 0:
            row = lax.broadcasted_iota(jnp.int32, other.shape, 1)
            identity = jnp.where(row < size, 0.0, 1.0).astype(jnp.float32)
            state[r] = jnp.where(has_input, other, identity)
        else:
            mine = state[r - 1]
            fade = mine[:, size : size + 1, :]
            combined_state = fade * other[:, :size, :] + mine[:, :size, :]
            combined_fade = mine[:, size:, :] * other[:, size:, :]
            state[r, :, :size, :] = jnp.where(has_input, combined_state, mine[:, :size, :])
            state[r, :, size:, :] = jnp.where(has_input, combined_fade, mine[:, size:, :])

    o_ref[...] = state[len(shifts) - 1, :, :size, :]


def incoming_state(packed):
    heads, rows, width = packed.shape
    steps = 4
    return pl.pallas_call(
        scan_kernel,
        out_shape=jax.ShapeDtypeStruct((heads, rows - 8, width), jnp.float32),
        in_specs=[pl.BlockSpec(memory_space=pltpu.VMEM)],
        out_specs=pl.BlockSpec(memory_space=pltpu.VMEM),
        scratch_shapes=[
            pltpu.VMEM((steps, heads, rows, width), jnp.float32),
            pltpu.VMEM((steps, heads, rows, width), jnp.float32),
            pltpu.SemaphoreType.DMA((steps,)),
            pltpu.SemaphoreType.DMA((steps,)),
        ],
        compiler_params=pltpu.CompilerParams(collective_id=2, has_side_effects=True),
    )(packed)


def on_device(
    attn_query,
    attn_key,
    attn_value,
    log_decay,
    residual,
    norm_gain,
    expert_ids,
    router_weight,
    gate_weight,
    up_weight,
    down_weight,
):
    heads_here = log_decay.shape[0]
    length = log_decay.shape[1]
    head_size = attn_query.shape[1] // heads_here
    query_rows = attn_query.reshape(length, heads_here, head_size)
    key_rows = attn_key.reshape(length, heads_here, head_size)
    value_rows = attn_value.reshape(length, heads_here, head_size)
    cumulative = jnp.cumsum(log_decay, axis=1)
    causal = lax.broadcasted_iota(jnp.int32, (length, length), 0) >= lax.broadcasted_iota(
        jnp.int32, (length, length), 1
    )
    decay_gap = jnp.where(causal[None], cumulative[:, :, None] - cumulative[:, None, :], 0.0)
    decay_mask = jnp.where(causal[None], jnp.exp(decay_gap), 0.0)
    scores = jnp.einsum("thd,shd->hts", query_rows, key_rows, preferred_element_type=jnp.float32)
    weights = (scores * decay_mask).astype(jnp.bfloat16)
    intra_part = jnp.einsum("hts,shd->thd", weights, value_rows, preferred_element_type=jnp.float32)
    key_fade = jnp.exp(cumulative[:, -1:] - cumulative)
    scaled = (key_fade.T[:, :, None] * key_rows.astype(jnp.float32)).astype(jnp.bfloat16)
    local_state = jnp.einsum("shd,she->hde", scaled, value_rows, preferred_element_type=jnp.float32)
    section_fade = jnp.exp(cumulative[:, -1])
    packed = jnp.concatenate(
        [local_state, jnp.broadcast_to(section_fade[:, None, None], (heads_here, 8, head_size))],
        axis=1,
    )
    incoming = incoming_state(packed)
    inter_part = jnp.einsum(
        "thd,hde->the", query_rows.astype(jnp.float32), incoming, precision=lax.Precision.HIGHEST
    )
    attn_out = intra_part + jnp.exp(cumulative).T[:, :, None] * inter_part
    mean_square = jnp.mean(attn_out * attn_out, axis=2, keepdims=True)
    normed = (attn_out / jnp.sqrt(mean_square + 1e-06)).reshape(length, heads_here * head_size)
    stream = (residual.astype(jnp.float32) + norm_gain.astype(jnp.float32) * normed).astype(
        jnp.bfloat16
    )
    experts_here = router_weight.shape[1]
    groups = lax.axis_size("seq")
    expert_count = experts_here * groups
    capacity = 4 * length // expert_count
    features = stream.shape[1]
    choices_per_token = expert_ids.shape[1]
    flat_ids = expert_ids.reshape(-1)
    expert_iota = lax.broadcasted_iota(jnp.int32, (1, expert_count), 1)
    onehot = (flat_ids[:, None] == expert_iota).astype(jnp.int32)
    running = jnp.cumsum(onehot, axis=0)
    slot_index = jnp.sum(running * onehot, axis=1) - 1
    target = flat_ids * capacity + slot_index
    place_iota = lax.broadcasted_iota(jnp.int32, (expert_count * capacity, 1), 0)
    route_matrix = (
        (place_iota == target[None, :])
        .astype(jnp.bfloat16)
        .reshape(expert_count * capacity, length, choices_per_token)
        .sum(axis=2)
    )
    outgoing = jnp.dot(route_matrix, stream, preferred_element_type=jnp.float32).astype(
        jnp.bfloat16
    )
    outgoing = outgoing.reshape(groups, experts_here, capacity, features)
    shards = lax.axis_size("exp")
    portion = lax.all_gather(
        exchange(outgoing, 0),
        "exp",
        axis=0,
    )
    hidden_units = gate_weight.shape[2]
    gate_blocks = gate_weight.reshape(experts_here, shards, features, hidden_units)
    up_blocks = up_weight.reshape(experts_here, shards, features, hidden_units)
    router_blocks = router_weight.reshape(shards, features, experts_here)
    gate_up = jnp.einsum(
        "esjcd,jedf->sjcf",
        portion,
        jnp.concatenate([gate_blocks, up_blocks], axis=3),
        preferred_element_type=jnp.float32,
    )
    gate_acc = gate_up[..., :hidden_units]
    upward = gate_up[..., hidden_units:]
    logits = jnp.einsum(
        "esjcd,edj->sjc", portion, router_blocks, preferred_element_type=jnp.float32
    )
    hidden_act = (jax.nn.silu(gate_acc) * upward).astype(jnp.bfloat16)
    expert_out = lax.psum_scatter(
        down_projection(hidden_act, down_weight, shards),
        "exp",
        scatter_dimension=0,
        tiled=True,
    )[0].astype(jnp.float32)
    routed = (jax.nn.sigmoid(logits)[..., None] * expert_out).astype(jnp.bfloat16)
    returned = exchange(routed, 1)
    returned = returned.reshape(expert_count * capacity, features)
    combined = lax.dot_general(
        route_matrix, returned, (((0,), (0,)), ((), ())), preferred_element_type=jnp.float32
    )
    return (stream.astype(jnp.float32) + combined).astype(jnp.bfloat16)


def solution(mesh):
    in_specs = (
        P("seq", "exp"),
        P("seq", "exp"),
        P("seq", "exp"),
        P("exp", "seq"),
        P("seq", "exp"),
        P("exp"),
        P("seq", None),
        P(None, "seq"),
        P("seq", None, "exp"),
        P("seq", None, "exp"),
        P("seq", "exp", None),
    )
    out_specs = P("seq", "exp")
    return jax.shard_map(
        on_device, mesh=mesh, in_specs=in_specs, out_specs=out_specs, check_vma=False
    )
```

```python
import functools

import jax
import jax.numpy as jnp
from jax import lax
from jax.sharding import PartitionSpec as P
from jax.experimental import pallas as pl
from jax.experimental.pallas import tpu as pltpu


def shifted(array, axis, by):
    count = lax.axis_size(axis)
    pairs = [(i, i + by) for i in range(count) if 0 <= i + by < count]
    return lax.ppermute(array, axis, pairs)


def down_kernel(blocks_per_step, block_width, h_ref, w_ref, o_ref):
    sections, capacity, both = h_ref.shape
    hidden = both // 2
    pair = h_ref[...].reshape(sections * capacity, both)
    gate_acc = pair[:, :hidden]
    rows = (gate_acc / (1.0 + jnp.exp(-gate_acc)) * pair[:, hidden:]).astype(jnp.bfloat16)
    product = jnp.dot(rows, w_ref[...], preferred_element_type=jnp.float32)
    for i in range(blocks_per_step):
        piece = product[:, i * block_width : (i + 1) * block_width]
        o_ref[i] = piece.astype(o_ref.dtype).reshape(sections, capacity, block_width)


def down_projection(hidden_act, down_weight, shards):
    sections, experts_here, capacity, both = hidden_act.shape
    hidden = both // 2
    features = down_weight.shape[2]
    block_width = features // shards
    blocks_per_step = 8
    steps = shards // blocks_per_step
    return pl.pallas_call(
        functools.partial(down_kernel, blocks_per_step, block_width),
        out_shape=jax.ShapeDtypeStruct(
            (shards, sections, experts_here, capacity, block_width), jnp.bfloat16
        ),
        grid=(experts_here, steps),
        in_specs=[
            pl.BlockSpec((sections, None, capacity, both), lambda j, b: (0, j, 0, 0)),
            pl.BlockSpec((None, hidden, blocks_per_step * block_width), lambda j, b: (j, 0, b)),
        ],
        out_specs=pl.BlockSpec(
            (blocks_per_step, sections, None, capacity, block_width),
            lambda j, b: (b, 0, j, 0, 0),
        ),
        cost_estimate=pl.CostEstimate(
            flops=2 * sections * experts_here * capacity * hidden * features,
            bytes_accessed=4 * hidden_act.size + 2 * (down_weight.size + hidden_act.size // both * features),
            transcendentals=0,
        ),
    )(hidden_act, down_weight)


def exchange_kernel(x_ref, o_ref, send_sem, recv_sem, local_sem):
    n = x_ref.shape[0]
    me = lax.axis_index("seq")
    col = lax.axis_index("exp")
    mesh_id = pl.DeviceIdType.MESH
    barrier = pltpu.get_barrier_semaphore()
    for k in range(1, n):
        peer = lax.rem(me + k, n)
        pl.semaphore_signal(barrier, inc=1, device_id=(peer, col), device_id_type=mesh_id)
    pl.semaphore_wait(barrier, n - 1)
    local = pltpu.make_async_copy(x_ref.at[me], o_ref.at[me], local_sem)
    local.start()
    copies = []
    for k in range(1, n):
        peer = lax.rem(me + k, n)
        copy = pltpu.make_async_remote_copy(
            src_ref=x_ref.at[peer],
            dst_ref=o_ref.at[me],
            send_sem=send_sem.at[k],
            recv_sem=recv_sem.at[k],
            device_id=(peer, col),
            device_id_type=mesh_id,
        )
        copy.start()
        copies.append(copy)
    local.wait()
    for copy in copies:
        copy.wait()


def exchange(x, collective_id):
    n = x.shape[0]
    return pl.pallas_call(
        exchange_kernel,
        out_shape=jax.ShapeDtypeStruct(x.shape, x.dtype),
        in_specs=[pl.BlockSpec(memory_space=pltpu.VMEM)],
        out_specs=pl.BlockSpec(memory_space=pltpu.VMEM),
        scratch_shapes=[
            pltpu.SemaphoreType.DMA((n,)),
            pltpu.SemaphoreType.DMA((n,)),
            pltpu.SemaphoreType.DMA,
        ],
        compiler_params=pltpu.CompilerParams(collective_id=collective_id, has_side_effects=True),
    )(x)


def scan_kernel(x_ref, o_ref, state, received, send_sem, recv_sem):
    n = lax.axis_size("seq")
    me = lax.axis_index("seq")
    col = lax.axis_index("exp")
    mesh_id = pl.DeviceIdType.MESH
    size = x_ref.shape[1] - 8
    barrier = pltpu.get_barrier_semaphore()
    for k in range(1, n):
        peer = lax.rem(me + k, n)
        pl.semaphore_signal(barrier, inc=1, device_id=(peer, col), device_id_type=mesh_id)
    pl.semaphore_wait(barrier, n - 1)
    shifts = [1, 1, 2, 4]
    for r, d in enumerate(shifts):
        source = x_ref if r == 0 else state.at[r - 1]
        copy = pltpu.make_async_remote_copy(
            src_ref=source,
            dst_ref=received.at[r],
            send_sem=send_sem.at[r],
            recv_sem=recv_sem.at[r],
            device_id=(lax.rem(me + d, n), col),
            device_id_type=mesh_id,
        )
        copy.start()
        copy.wait()
        has_input = me - d >= 0
        other = received[r]
        if r == 0:
            row = lax.broadcasted_iota(jnp.int32, other.shape, 1)
            identity = jnp.where(row < size, 0.0, 1.0).astype(jnp.float32)
            state[r] = jnp.where(has_input, other, identity)
        else:
            mine = state[r - 1]
            fade = mine[:, size : size + 1, :]
            combined_state = fade * other[:, :size, :] + mine[:, :size, :]
            combined_fade = mine[:, size:, :] * other[:, size:, :]
            state[r, :, :size, :] = jnp.where(has_input, combined_state, mine[:, :size, :])
            state[r, :, size:, :] = jnp.where(has_input, combined_fade, mine[:, size:, :])

    o_ref[...] = state[len(shifts) - 1, :, :size, :]


def incoming_state(packed):
    heads, rows, width = packed.shape
    steps = 4
    return pl.pallas_call(
        scan_kernel,
        out_shape=jax.ShapeDtypeStruct((heads, rows - 8, width), jnp.float32),
        in_specs=[pl.BlockSpec(memory_space=pltpu.VMEM)],
        out_specs=pl.BlockSpec(memory_space=pltpu.VMEM),
        scratch_shapes=[
            pltpu.VMEM((steps, heads, rows, width), jnp.float32),
            pltpu.VMEM((steps, heads, rows, width), jnp.float32),
            pltpu.SemaphoreType.DMA((steps,)),
            pltpu.SemaphoreType.DMA((steps,)),
        ],
        compiler_params=pltpu.CompilerParams(collective_id=2, has_side_effects=True),
    )(packed)


def on_device(
    attn_query,
    attn_key,
    attn_value,
    log_decay,
    residual,
    norm_gain,
    expert_ids,
    router_weight,
    gate_weight,
    up_weight,
    down_weight,
):
    heads_here = log_decay.shape[0]
    length = log_decay.shape[1]
    head_size = attn_query.shape[1] // heads_here
    query_rows = attn_query.reshape(length, heads_here, head_size)
    key_rows = attn_key.reshape(length, heads_here, head_size)
    value_rows = attn_value.reshape(length, heads_here, head_size)
    cumulative = jnp.cumsum(log_decay, axis=1)
    causal = lax.broadcasted_iota(jnp.int32, (length, length), 0) >= lax.broadcasted_iota(
        jnp.int32, (length, length), 1
    )
    decay_gap = jnp.where(causal[None], cumulative[:, :, None] - cumulative[:, None, :], 0.0)
    decay_mask = jnp.where(causal[None], jnp.exp(decay_gap), 0.0)
    scores = jnp.einsum("thd,shd->hts", query_rows, key_rows, preferred_element_type=jnp.float32)
    weights = (scores * decay_mask).astype(jnp.bfloat16)
    intra_part = jnp.einsum("hts,shd->thd", weights, value_rows, preferred_element_type=jnp.float32)
    key_fade = jnp.exp(cumulative[:, -1:] - cumulative)
    scaled = (key_fade.T[:, :, None] * key_rows.astype(jnp.float32)).astype(jnp.bfloat16)
    local_state = jnp.einsum("shd,she->hde", scaled, value_rows, preferred_element_type=jnp.float32)
    section_fade = jnp.exp(cumulative[:, -1])
    packed = jnp.concatenate(
        [local_state, jnp.broadcast_to(section_fade[:, None, None], (heads_here, 8, head_size))],
        axis=1,
    )
    incoming = incoming_state(packed)
    inter_part = jnp.einsum(
        "thd,hde->the", query_rows.astype(jnp.float32), incoming, precision=lax.Precision.HIGHEST
    )
    attn_out = intra_part + jnp.exp(cumulative).T[:, :, None] * inter_part
    mean_square = jnp.mean(attn_out * attn_out, axis=2, keepdims=True)
    normed = (attn_out / jnp.sqrt(mean_square + 1e-06)).reshape(length, heads_here * head_size)
    stream = (residual.astype(jnp.float32) + norm_gain.astype(jnp.float32) * normed).astype(
        jnp.bfloat16
    )
    experts_here = router_weight.shape[1]
    groups = lax.axis_size("seq")
    expert_count = experts_here * groups
    capacity = 4 * length // expert_count
    features = stream.shape[1]
    choices_per_token = expert_ids.shape[1]
    flat_ids = expert_ids.reshape(-1)
    expert_iota = lax.broadcasted_iota(jnp.int32, (1, expert_count), 1)
    onehot = (flat_ids[:, None] == expert_iota).astype(jnp.int32)
    running = jnp.cumsum(onehot, axis=0)
    slot_index = jnp.sum(running * onehot, axis=1) - 1
    target = flat_ids * capacity + slot_index
    place_iota = lax.broadcasted_iota(jnp.int32, (expert_count * capacity, 1), 0)
    route_matrix = (
        (place_iota == target[None, :])
        .astype(jnp.bfloat16)
        .reshape(expert_count * capacity, length, choices_per_token)
        .sum(axis=2)
    )
    outgoing = jnp.dot(route_matrix, stream, preferred_element_type=jnp.float32).astype(
        jnp.bfloat16
    )
    outgoing = outgoing.reshape(groups, experts_here, capacity, features)
    shards = lax.axis_size("exp")
    portion = lax.all_gather(
        exchange(outgoing, 0),
        "exp",
        axis=0,
    )
    hidden_units = gate_weight.shape[2]
    gate_blocks = gate_weight.reshape(experts_here, shards, features, hidden_units)
    up_blocks = up_weight.reshape(experts_here, shards, features, hidden_units)
    router_blocks = router_weight.reshape(shards, features, experts_here)
    gate_up = jnp.einsum(
        "esjcd,jedf->sjcf",
        portion,
        jnp.concatenate([gate_blocks, up_blocks], axis=3),
        preferred_element_type=jnp.float32,
    )
    logits = jnp.einsum(
        "esjcd,edj->sjc", portion, router_blocks, preferred_element_type=jnp.float32
    )
    expert_out = lax.psum_scatter(
        down_projection(gate_up, down_weight, shards),
        "exp",
        scatter_dimension=0,
        tiled=True,
    )[0].astype(jnp.float32)
    routed = (jax.nn.sigmoid(logits)[..., None] * expert_out).astype(jnp.bfloat16)
    returned = exchange(routed, 1)
    returned = returned.reshape(expert_count * capacity, features)
    combined = lax.dot_general(
        route_matrix, returned, (((0,), (0,)), ((), ())), preferred_element_type=jnp.float32
    )
    return (stream.astype(jnp.float32) + combined).astype(jnp.bfloat16)


def solution(mesh):
    in_specs = (
        P("seq", "exp"),
        P("seq", "exp"),
        P("seq", "exp"),
        P("exp", "seq"),
        P("seq", "exp"),
        P("exp"),
        P("seq", None),
        P(None, "seq"),
        P("seq", None, "exp"),
        P("seq", None, "exp"),
        P("seq", "exp", None),
    )
    out_specs = P("seq", "exp")
    return jax.shard_map(
        on_device, mesh=mesh, in_specs=in_specs, out_specs=out_specs, check_vma=False
    )
```
